32 devices in a mesh: rows: 4 (over x, core), cols: 2 (over y), heads: 4 (over z).
Axes of the slice: x: 2, y: 2, z: 4, core: 2. Of those that a mesh axis runs over, the one named last changes fastest.
Arguments:
- latent: bfloat16 [3, 4, 128, 64], P(None, None, 'rows', 'cols'), may hold values from -6 to 6
- skip_in: bfloat16 [3, 64, 32, 1408], P(None, 'rows', 'cols'), may hold values from -6 to 6
- context: bfloat16 [6, 333, 1024], replicated, may hold values from -6 to 6
- image_ids: int32 [3, 64, 32], P(None, 'rows', 'cols'), may hold values from 0 to 5, as said below
- text_mask: int32 [6, 333], replicated, may hold values from 0 to 1, as said below
- patch_weight: bfloat16 [16, 1408], replicated, may hold values from -1.5 to 1.5
- skip_gain: float32 [2816], replicated, may hold values from 0.1 to 1.9
- skip_weight: bfloat16 [2816, 1408], replicated, may hold values from -0.109375 to 0.109375
- norm_gains: float32 [3, 1408], replicated, may hold values from 0.1 to 1.9
- qkv_weight: bfloat16 [3, 1408, 1408], P(None, None, 'heads'), may hold values from -0.15625 to 0.15625
- qk_gains: float32 [4, 88], replicated, may hold values from 0.1 to 1.9
- out_weight: bfloat16 [1408, 1408], P('heads'), may hold values from -3 to 3
- cq_weight: bfloat16 [1408, 1408], P(None, 'heads'), may hold values from -0.15625 to 0.15625
- ckv_weight: bfloat16 [2, 1024, 1408], P(None, None, 'heads'), may hold values from -0.1875 to 0.1875
- cout_weight: bfloat16 [1408, 1408], P('heads'), may hold values from -1.25 to 1.25
- up_weight: bfloat16 [1408, 6144], P(None, 'heads'), may hold values from -0.15625 to 0.15625
- down_weight: bfloat16 [6144, 1408], P('heads'), may hold values from -0.078125 to 0.078125
- final_weight: bfloat16 [1408, 32], replicated, may hold values from -0.15625 to 0.15625
- cotangent: bfloat16 [3, 8, 128, 64], P(None, None, 'rows', 'cols'), may hold values from -6 to 6
Outputs:
- out_latent: bfloat16 [3, 8, 128, 64], P(None, None, 'rows', 'cols')
- grad_latent: bfloat16 [3, 4, 128, 64], P(None, None, 'rows', 'cols')
- grad_skip: bfloat16 [3, 64, 32, 1408], P(None, 'rows', 'cols')
- grad_patch_weight: float32 [16, 1408], P(None, ('rows', 'cols'))
- grad_skip_gain: float32 [2816], replicated
- grad_skip_weight: float32 [2816, 1408], P(('rows', 'cols'))
- grad_norm_gains: float32 [3, 1408], replicated
- grad_qkv_weight: float32 [3, 1408, 1408], P(None, ('rows', 'cols'), 'heads')
- grad_qk_gains: float32 [4, 88], replicated
- grad_out_weight: float32 [1408, 1408], P('heads', ('rows', 'cols'))
- grad_cq_weight: float32 [1408, 1408], P(('rows', 'cols'), 'heads')
- grad_ckv_weight: float32 [2, 1024, 1408], P(None, ('rows', 'cols'), 'heads')
- grad_cout_weight: float32 [1408, 1408], P('heads', ('rows', 'cols'))
- grad_up_weight: float32 [1408, 6144], P(('rows', 'cols'), 'heads')
- grad_down_weight: float32 [6144, 1408], P('heads', ('rows', 'cols'))
- grad_final_weight: float32 [1408, 32], P(('rows', 'cols'))
The draws below stay inside these ranges and needn't reach their ends.
Inputs may be any that keep to these rules, and one draw needn't show every extreme that they name: `image_ids`: each aligned square of 32 x 32 patches of a pack (first row and column multiples of 32) carries one id, different squares carry different ids, and every id 0 to 5 is used once; the id also names the image's caption. `text_mask`: for each caption the first L1 of its 77 CLIP positions and the first L2 of its 256 mT5 positions are 1 and the rest 0, with L1 and L2 at least 1.
All inputs are finite; a program needn't handle non-finite values.
Results may differ from the reference program's by a relative error of at most 0.022.
Values may be sent and summed in bfloat16 or wider, within the bound.
No kernel may reach another device: no remote copies, remote signals or barrier semaphores. Data moves between devices by JAX's collectives and lax.ppermute only.
A program may use at most 256 MiB of HBM per device.

```python
import math
import jax
import jax.numpy as jnp
from jax import lax

D = 1408
HEADS = 16
HD = 88
FF = 6144
CTX = 1024
CLIP_LEN = 77
T5_LEN = 256
CH = 4
OC = 8
IMG = 32
PACKS = 3
GRID_R = 64
GRID_C = 32
LAT_R = 128
LAT_C = 64
IMAGES = 6
TXT = 333


def draw_image_ids(key, part):
    squares_r = GRID_R // IMG
    squares_c = GRID_C // IMG
    order = jax.random.permutation(key, IMAGES).reshape(PACKS, squares_r, squares_c)
    spread_ids = jnp.repeat(jnp.repeat(order, IMG, axis=1), IMG, axis=2)
    return spread_ids.astype(jnp.int32)


def draw_text_mask(key, part):
    first_key = jax.random.fold_in(key, 11)
    second_key = jax.random.fold_in(key, 23)
    clip_count = jax.random.randint(first_key, (IMAGES, 1), 1, CLIP_LEN + 1)
    mt5_count = jax.random.randint(second_key, (IMAGES, 1), 1, T5_LEN + 1)
    position = jnp.arange(TXT, dtype=jnp.int32)[None, :]
    present = (position < clip_count) | (position >= CLIP_LEN) & (position < CLIP_LEN + mt5_count)
    return present.astype(jnp.int32)


def levels(own_key, shape, shards, least, top_value):
    loudness = 1.0
    for axis_at, shards_of in shards:
        heights = jax.random.uniform(jax.random.fold_in(jax.random.fold_in(own_key, 6), axis_at), (shards_of,), jnp.float32, least / len(shards), top_value / len(shards))
        loudness = loudness * jnp.repeat(jnp.exp(heights), shape[axis_at] // shards_of).reshape((-1,) + (1,) * (len(shape) - 1 - axis_at))
    return loudness


def centred(rng, extent, scale, bound, split=(), kind=jnp.bfloat16):
    values = scale * jax.random.normal(rng, extent, jnp.float32)
    if split:
        values = values * levels(rng, extent, split, -0.22, 0.18)
    return jnp.clip(values, -bound, bound).astype(kind)


def setup_inputs(seed: int = 0) -> dict:
    streams_of = jax.random.split(jax.random.key(seed), 20)
    latent = centred(streams_of[0], (PACKS, CH, LAT_R, LAT_C), 1.0, 6.0, ((2, 4), (3, 2)))
    skip_in = centred(streams_of[1], (PACKS, GRID_R, GRID_C, D), 1.0, 6.0, ((1, 4), (2, 2)))
    context = centred(streams_of[2], (IMAGES, TXT, CTX), 1.0, 6.0)
    image_ids = draw_image_ids(jax.random.fold_in(streams_of[19], 71), 0)
    text_mask = draw_text_mask(jax.random.fold_in(streams_of[19], 71), 0)
    patch_weight = centred(streams_of[5], (4 * CH, D), (4 * CH) ** -0.5, 1.5)
    skip_gain = jnp.clip(1.0 + 0.18 * jax.random.normal(streams_of[6], (2 * D,), jnp.float32), 0.1, 1.9)
    skip_weight = centred(streams_of[7], (2 * D, D), (2 * D) ** -0.5, 0.109375)
    norm_gains = jnp.clip(1.0 + 0.18 * jax.random.normal(streams_of[8], (3, D), jnp.float32), 0.1, 1.9)
    qkv_weight = centred(streams_of[9], (3, D, HEADS * HD), D ** -0.5, 0.15625, ((2, 4),))
    qk_gains = jnp.clip(1.0 + 0.18 * jax.random.normal(streams_of[10], (4, HD), jnp.float32), 0.1, 1.9)
    out_weight = centred(streams_of[11], (HEADS * HD, D), 4 ** -0.5, 3.0, ((0, 4),))
    cq_weight = centred(streams_of[12], (D, HEADS * HD), D ** -0.5, 0.15625, ((1, 4),))
    ckv_weight = centred(streams_of[13], (2, CTX, HEADS * HD), CTX ** -0.5, 0.1875, ((2, 4),))
    cout_weight = centred(streams_of[14], (HEADS * HD, D), 24 ** -0.5, 1.25, ((0, 4),))
    up_weight = centred(streams_of[15], (D, FF), D ** -0.5, 0.15625, ((1, 4),))
    down_weight = centred(streams_of[16], (FF, D), FF ** -0.5, 0.078125, ((0, 4),))
    final_weight = centred(streams_of[17], (D, 4 * OC), D ** -0.5, 0.15625)
    cotangent = centred(streams_of[18], (PACKS, OC, LAT_R, LAT_C), 1.0, 6.0, ((2, 4), (3, 2)))
    return dict(latent=latent, skip_in=skip_in, context=context, image_ids=image_ids, text_mask=text_mask, patch_weight=patch_weight, skip_gain=skip_gain, skip_weight=skip_weight, norm_gains=norm_gains, qkv_weight=qkv_weight, qk_gains=qk_gains, out_weight=out_weight, cq_weight=cq_weight, ckv_weight=ckv_weight, cout_weight=cout_weight, up_weight=up_weight, down_weight=down_weight, final_weight=final_weight, cotangent=cotangent)


EPSILON = 1e-06
HIGHEST = lax.Precision.HIGHEST

@jax.custom_vjp
def low(v):
    return lax.optimization_barrier(v.astype(jnp.bfloat16)).astype(jnp.float32)

@jax.custom_vjp
def low_back(v):
    return v

def low_keep(v):
    return (low(v), None)

def low_pass(kept, grad):
    return (grad,)

def back_keep(v):
    return (v, None)

def back_low(kept, grad):
    return (low(grad),)
low.defvjp(low_keep, low_pass)
low_back.defvjp(back_keep, back_low)

def norm_rows(values):
    center = values - lax.optimization_barrier(jnp.mean(values, -1, keepdims=True))
    spread = lax.optimization_barrier(jnp.mean(center * center, -1, keepdims=True))
    return center * lax.rsqrt(spread + EPSILON)

def matmul_high(left, right):
    return jnp.matmul(left, right, precision=HIGHEST)

def patchify(pixels):
    pack_count, channels, lat_rows, lat_cols = pixels.shape
    padded = jnp.pad(pixels, ((0, 0), (0, 0), (0, 1), (0, 1)))[:, :, 1:, 1:]
    padded = padded.reshape(pack_count, channels, lat_rows // 2, 2, lat_cols // 2, 2)
    padded = padded.transpose(0, 2, 4, 1, 3, 5)
    return padded.reshape(pack_count, lat_rows // 2 * (lat_cols // 2), channels * 4)

def unpatchify(tokens, grid_rows, grid_cols):
    pack_count = tokens.shape[0]
    channels = tokens.shape[2] // 4
    pixels = tokens.reshape(pack_count, grid_rows, grid_cols, channels, 2, 2).transpose(0, 3, 1, 4, 2, 5)
    pixels = pixels.reshape(pack_count, channels, 2 * grid_rows, 2 * grid_cols)
    return jnp.pad(pixels, ((0, 0), (0, 0), (1, 0), (1, 0)))[:, :, :-1, :-1]

def partner(values):
    quarter = values.shape[-1] // 4
    return jnp.concatenate([-values[..., quarter:2 * quarter], values[..., :quarter], -values[..., 3 * quarter:], values[..., 2 * quarter:3 * quarter]], -1)

def rope_tables(row_pos, col_pos, head_dim):
    quarter = head_dim // 4
    freqs = 10000.0 ** (-jnp.arange(quarter, dtype=jnp.float32) / quarter)
    row_angle = row_pos.astype(jnp.float32)[:, None] * freqs[None, :]
    col_angle = col_pos.astype(jnp.float32)[:, None] * freqs[None, :]
    cosine = jnp.concatenate([jnp.cos(row_angle), jnp.cos(row_angle), jnp.cos(col_angle), jnp.cos(col_angle)], -1)
    sine = jnp.concatenate([jnp.sin(row_angle), jnp.sin(row_angle), jnp.sin(col_angle), jnp.sin(col_angle)], -1)
    return (cosine, sine)

def attend(queries, keys_all, values_all, allowed):
    scaling = 1.0 / math.sqrt(queries.shape[-1])
    scores = jnp.einsum('bhe,khe->hbk', queries, keys_all, precision=HIGHEST) * scaling
    scores = low_back(scores)
    scores = jnp.where(allowed[None], scores, -1e+30)
    weights_soft = low(jax.nn.softmax(scores, axis=-1))
    return jnp.einsum('hbk,khe->bhe', weights_soft, values_all, precision=HIGHEST)

def attend_blocks(queries, keys_all, values_all, query_ids, key_ids, key_valid):
    row_total = queries.shape[0]
    block_size = math.gcd(row_total, 512)
    query_blocks = queries.reshape(row_total // block_size, block_size, queries.shape[1], queries.shape[2])
    id_blocks = query_ids.reshape(row_total // block_size, block_size)

    def one_block(block_pair):
        block_queries, block_ids = block_pair
        allowed = (block_ids[:, None] == key_ids[None, :]) & (key_valid[None, :] > 0)
        return attend(block_queries, keys_all, values_all, allowed)
    mixture = lax.map(jax.checkpoint(one_block), (query_blocks, id_blocks))
    return mixture.reshape(queries.shape)

def layer(latent, skip_in, patch_weight, skip_gain, skip_weight, norm_gains, qkv_weight, qk_gains, out_weight, cq_weight, ckv_weight, cout_weight, up_weight, down_weight, final_weight, context, image_ids, text_mask):
    pack_count = latent.shape[0]
    grid_rows = latent.shape[2] // 2
    grid_cols = latent.shape[3] // 2
    cells = grid_rows * grid_cols
    model_width = skip_weight.shape[1]
    head_dim = qk_gains.shape[1]
    head_count = qkv_weight.shape[2] // head_dim
    captions = context.shape[0]
    text_len = context.shape[1]
    patches = patchify(latent)
    embed = low_back(matmul_high(patches, patch_weight))
    joined = jnp.concatenate([embed, skip_in.reshape(pack_count, cells, model_width)], -1)
    normed = low(norm_rows(joined) * skip_gain)
    hidden = low_back(matmul_high(normed, skip_weight))
    n_one = low(norm_rows(hidden) * norm_gains[0])
    projected = low_back(jnp.einsum('pnd,sde->spne', n_one, qkv_weight, precision=HIGHEST))
    projected = projected.reshape(3, pack_count, cells, head_count, head_dim)
    token_index = jnp.arange(cells, dtype=jnp.int32)
    row_pos = token_index // grid_cols % IMG
    col_pos = token_index % grid_cols % IMG
    cosine, sine = rope_tables(row_pos, col_pos, head_dim)
    cosine = cosine[:, None, :]
    sine = sine[:, None, :]

    def rotated(values, gain):
        scaled = norm_rows(values) * gain
        return scaled * cosine + partner(scaled) * sine
    queries = low(rotated(projected[0], qk_gains[0]))
    keys_self = low(rotated(projected[1], qk_gains[1]))
    values_self = low(projected[2])
    flat_ids = image_ids.reshape(pack_count, cells)
    all_valid = jnp.ones((cells,), jnp.int32)
    mixture = jnp.stack([attend_blocks(queries[pack_index], keys_self[pack_index], values_self[pack_index], flat_ids[pack_index], flat_ids[pack_index], all_valid) for pack_index in range(pack_count)])
    mixture = low_back(low(mixture.reshape(pack_count, cells, head_count * head_dim)))
    x_one = hidden + low_back(matmul_high(mixture, out_weight))
    n_two = low(norm_rows(x_one) * norm_gains[1])
    cq_pre = low_back(matmul_high(n_two, cq_weight)).reshape(pack_count, cells, head_count, head_dim)
    cross_queries = low(norm_rows(cq_pre) * qk_gains[2])
    ckv_pre = low_back(jnp.einsum('mtc,sce->smte', context, ckv_weight, precision=HIGHEST))
    ckv_pre = ckv_pre.reshape(2, captions * text_len, head_count, head_dim)
    cross_keys = low(norm_rows(ckv_pre[0]) * qk_gains[3])
    cross_values = low(ckv_pre[1])
    key_ids = jnp.repeat(jnp.arange(captions, dtype=jnp.int32), text_len)
    key_valid = text_mask.reshape(captions * text_len)
    cross_mix = jnp.stack([attend_blocks(cross_queries[pack_index], cross_keys, cross_values, flat_ids[pack_index], key_ids, key_valid) for pack_index in range(pack_count)])
    cross_mix = low_back(low(cross_mix.reshape(pack_count, cells, head_count * head_dim)))
    x_two = x_one + low_back(matmul_high(cross_mix, cout_weight))
    n_three = low(norm_rows(x_two) * norm_gains[2])
    up_pre = low_back(matmul_high(n_three, up_weight))
    activated = low(jax.nn.gelu(up_pre, approximate=True))
    x_three = x_two + low_back(matmul_high(activated, down_weight))
    n_four = low(norm_rows(x_three))
    return unpatchify(matmul_high(n_four, final_weight), grid_rows, grid_cols)

def reference(latent, skip_in, context, image_ids, text_mask, patch_weight, skip_gain, skip_weight, norm_gains, qkv_weight, qk_gains, out_weight, cq_weight, ckv_weight, cout_weight, up_weight, down_weight, final_weight, cotangent):
    text_float = context.astype(jnp.float32)

    def run(lat, skp, pw, sg, sw, ng, qw, qg, ow, cqw, ckw, cow, uw, dw, fw):
        return layer(lat, skp, pw, sg, sw, ng, qw, qg, ow, cqw, ckw, cow, uw, dw, fw, text_float, image_ids, text_mask)
    output, pull = jax.vjp(run, latent.astype(jnp.float32), skip_in.astype(jnp.float32), patch_weight.astype(jnp.float32), skip_gain, skip_weight.astype(jnp.float32), norm_gains, qkv_weight.astype(jnp.float32), qk_gains, out_weight.astype(jnp.float32), cq_weight.astype(jnp.float32), ckv_weight.astype(jnp.float32), cout_weight.astype(jnp.float32), up_weight.astype(jnp.float32), down_weight.astype(jnp.float32), final_weight.astype(jnp.float32))
    grads = pull(cotangent.astype(jnp.float32))
    return (output.astype(jnp.bfloat16), grads[0].astype(jnp.bfloat16), grads[1].astype(jnp.bfloat16), grads[2], grads[3], grads[4], grads[5], grads[6], grads[7], grads[8], grads[9], grads[10], grads[11], grads[12], grads[13], grads[14])
```

```python
import functools
import math

import jax
import jax.numpy as jnp
from jax import lax
from jax.sharding import Mesh, PartitionSpec as P

EPSILON = 1e-06


TILES = ("x", "core", "chi", "clo")
SHARERS = ("x", "core", "clo")
EVERYONE = ("x", "core", "chi", "clo", "zh", "zl")


def swapped(value, axis):
    return lax.ppermute(value, axis, [(i, i ^ 1) for i in range(lax.axis_size(axis))])


def from_behind(value, axis, by):
    devices = math.prod(lax.axis_size(name) for name in axis)
    pairs = [(i, i + by) for i in range(devices) if 0 <= i + by < devices]
    return lax.ppermute(value, axis, pairs)


def pick(values, index, axis):
    return lax.dynamic_index_in_dim(values, index, axis, keepdims=False)


def partner_shard(weight):
    sharers = math.prod(lax.axis_size(axis) for axis in SHARERS)
    depth = weight.shape[0] // sharers
    piece = lax.dynamic_slice_in_dim(weight, lax.axis_index(SHARERS) * depth, depth, 0)
    return lax.all_gather(swapped(piece, "zh"), SHARERS, axis=0, tiled=True)


def pair_sum(partial):
    mine = lax.optimization_barrier(partial.astype(jnp.bfloat16))
    other = swapped(mine, "zl")
    return mine.astype(jnp.float32) + other.astype(jnp.float32)


def norm_rows(values):
    center = values - jnp.mean(values, -1, keepdims=True)
    spread = jnp.mean(center * center, -1, keepdims=True)
    return center * lax.rsqrt(spread + EPSILON)


def scaled_norm(values, gain):
    return norm_rows(values) * gain


def partner(values):
    quarter = values.shape[-1] // 4
    return jnp.concatenate(
        [
            -values[..., quarter : 2 * quarter],
            values[..., :quarter],
            -values[..., 3 * quarter :],
            values[..., 2 * quarter : 3 * quarter],
        ],
        -1,
    )


def rotated(values, gain, cosine, sine):
    scaled = norm_rows(values) * gain
    return scaled * cosine + partner(scaled) * sine


def rope_tables(row_pos, col_pos, head_dim):
    quarter = head_dim // 4
    freqs = 10000.0 ** (-jnp.arange(quarter, dtype=jnp.float32) / quarter)
    row_angle = row_pos.astype(jnp.float32)[:, None] * freqs[None, :]
    col_angle = col_pos.astype(jnp.float32)[:, None] * freqs[None, :]
    cosine = jnp.concatenate(
        [jnp.cos(row_angle), jnp.cos(row_angle), jnp.cos(col_angle), jnp.cos(col_angle)], -1
    )
    sine = jnp.concatenate(
        [jnp.sin(row_angle), jnp.sin(row_angle), jnp.sin(col_angle), jnp.sin(col_angle)], -1
    )
    return (cosine, sine)


def project(left, right):
    return jnp.dot(left, right, preferred_element_type=jnp.float32)


def outer_sum(left, right):
    return jnp.einsum("rd,re->de", left, right, preferred_element_type=jnp.float32)


def back_dot(grads, weight):
    return jnp.einsum("re,de->rd", grads, weight, preferred_element_type=jnp.float32)


def quadrant(block):
    from_rows = swapped(block, "core")
    paired = jnp.concatenate([block, from_rows], 2)
    from_cols = swapped(paired, "clo")
    return jnp.concatenate([paired, from_cols], 2)


def returned(grads, cells):
    paired = grads[:, :, : 2 * cells] + swapped(
        grads[:, :, 2 * cells :].astype(jnp.bfloat16), "clo"
    ).astype(jnp.float32)
    return paired[:, :, :cells] + swapped(
        paired[:, :, cells:].astype(jnp.bfloat16), "core"
    ).astype(jnp.float32)


def score_block(queries, keys_all, allowed):
    scaling = 1.0 / math.sqrt(queries.shape[-1])
    scores = (
        jnp.einsum("pqhe,pkhe->phqk", queries, keys_all, preferred_element_type=jnp.float32)
        * scaling
    )
    return jnp.where(allowed, scores, -1e30)


def forward_attention(queries, keys_all, values_all, allowed):
    scores = score_block(queries, keys_all, allowed)
    highest = jnp.max(scores, -1, keepdims=True)
    expo = jnp.exp(scores - highest)
    totals = jnp.sum(expo, -1, keepdims=True)
    weights_soft = (expo / totals).astype(jnp.bfloat16)
    mixture = jnp.einsum(
        "phqk,pkhe->pqhe", weights_soft, values_all, preferred_element_type=jnp.float32
    )
    return (mixture.astype(jnp.bfloat16), highest + jnp.log(totals))


def backward_attention(queries, keys_all, values_all, allowed, log_total, grad_mix):
    scaling = 1.0 / math.sqrt(queries.shape[-1])
    weights_soft = jnp.exp(score_block(queries, keys_all, allowed) - log_total)
    grad_weights = jnp.einsum(
        "pqhe,pkhe->phqk", grad_mix, values_all, preferred_element_type=jnp.float32
    )
    inner = jnp.sum(weights_soft * grad_weights, -1, keepdims=True)
    grad_scores = (weights_soft * (grad_weights - inner)).astype(jnp.bfloat16)
    grad_queries = (
        jnp.einsum("phqk,pkhe->pqhe", grad_scores, keys_all, preferred_element_type=jnp.float32)
        * scaling
    )
    grad_keys = (
        jnp.einsum("phqk,pqhe->pkhe", grad_scores, queries, preferred_element_type=jnp.float32)
        * scaling
    )
    grad_values = jnp.einsum(
        "phqk,pqhe->pkhe",
        weights_soft.astype(jnp.bfloat16),
        grad_mix,
        preferred_element_type=jnp.float32,
    )
    return (grad_queries, grad_keys, grad_values)


def shards(
    latent,
    skip_in,
    context,
    image_ids,
    text_mask,
    patch_weight,
    skip_gain,
    skip_weight,
    norm_gains,
    qkv_weight,
    qk_gains,
    out_weight,
    cq_weight,
    ckv_weight,
    cout_weight,
    up_weight,
    down_weight,
    final_weight,
    cotangent,
):
    pack_count = latent.shape[0]
    in_channels = latent.shape[1]
    out_channels = cotangent.shape[1]
    tile_side = image_ids.shape[1]
    cells = tile_side * tile_side
    row_total = pack_count * cells
    model_width = skip_weight.shape[1]
    head_dim = qk_gains.shape[1]
    head_width = qkv_weight.shape[2]
    local_heads = head_width // head_dim
    both_channels = in_channels + out_channels
    half_cells = cells // 2
    quarter_cells = cells // 4
    half_total = row_total // 2
    upper, lower = lax.axis_index("zh"), lax.axis_index("zl")
    out_other = partner_shard(out_weight)
    cq_other = partner_shard(cq_weight)
    text_width = context.shape[2]
    ckv_other = partner_shard(ckv_weight.reshape(2 * text_width, head_width)).reshape(ckv_weight.shape)
    cout_other = partner_shard(cout_weight)
    up_other = partner_shard(up_weight)
    down_other = partner_shard(down_weight)
    out_pair = (out_weight, out_other)
    cq_pair = (cq_weight, cq_other)
    ckv_pair = (ckv_weight, ckv_other)
    cout_pair = (cout_weight, cout_other)
    up_pair = (up_weight, up_other)
    down_pair = (down_weight, down_other)

    def my_half(values):
        shape = values.shape[1:]
        cut = pick(values.reshape(pack_count, 2, half_cells, *shape), upper, 1)
        return cut.reshape(half_total, *shape)

    def other_half(values):
        shape = values.shape[1:]
        cut = pick(values.reshape(pack_count, 2, half_cells, *shape), 1 - upper, 1)
        return cut.reshape(half_total, *shape)

    def both_halves(mine, other):
        shape = mine.shape[1:]
        mine = mine.reshape(pack_count, half_cells, *shape)
        other = other.reshape(pack_count, half_cells, *shape)
        first = jnp.where(upper == 0, mine, other)
        second = jnp.where(upper == 0, other, mine)
        return jnp.stack([first, second], 1).reshape(row_total, *shape)

    stacked = jnp.concatenate([latent, cotangent], 1)
    lower_rim = from_behind(stacked[:, :, :1, :], ("x", "core"), -1)
    stacked = jnp.concatenate([stacked, lower_rim], 2)
    right_rim = from_behind(stacked[:, :, :, :1], ("chi", "clo"), -1)
    stacked = jnp.concatenate([stacked, right_rim], 3)[:, :, 1:, 1:]
    pieces = stacked.reshape(pack_count, both_channels, tile_side, 2, tile_side, 2)
    pieces = pieces.transpose(0, 2, 4, 1, 3, 5).reshape(row_total, both_channels * 4)
    patches = pieces[:, : in_channels * 4]
    grad_result = my_half(pieces[:, in_channels * 4 :])
    token_index = jnp.arange(cells, dtype=jnp.int32)
    row_pos = lax.axis_index("core") * tile_side + token_index // tile_side
    col_pos = lax.axis_index("clo") * tile_side + token_index % tile_side
    cosine, sine = rope_tables(row_pos, col_pos, head_dim)
    cosine = cosine[None, :, None, :]
    sine = sine[None, :, None, :]
    turning = functools.partial(rotated, cosine=cosine, sine=sine)
    embed = project(patches, patch_weight)
    joined = jnp.concatenate(
        [embed, skip_in.reshape(row_total, model_width).astype(jnp.float32)], 1
    )
    normed = scaled_norm(joined, skip_gain).astype(jnp.bfloat16)
    hidden = project(normed, skip_weight)
    n_one = scaled_norm(hidden, norm_gains[0]).astype(jnp.bfloat16)
    projected = jnp.einsum("rd,sde->sre", n_one, qkv_weight, preferred_element_type=jnp.float32)
    projected = projected.reshape(3, pack_count, cells, local_heads, head_dim)
    queries = turning(projected[0], qk_gains[0]).astype(jnp.bfloat16)
    keys_own = turning(projected[1], qk_gains[1]).astype(jnp.bfloat16)
    values_own = projected[2].astype(jnp.bfloat16)
    nearby = quadrant(jnp.stack([keys_own, values_own]).reshape(2, pack_count, cells, head_width))
    near_keys = nearby[0].reshape(pack_count, 4 * cells, local_heads, head_dim)
    near_values = nearby[1].reshape(pack_count, 4 * cells, local_heads, head_dim)
    everywhere = jnp.ones((1, 1, 1, 1), jnp.bool_)
    mixture, self_total = forward_attention(queries, near_keys, near_values, everywhere)
    mixture = mixture.reshape(row_total, head_width)
    mix_pair = (my_half(mixture), swapped(other_half(mixture), "zh"))
    half_heads = (pack_count, half_cells, local_heads, head_dim)

    def joint(lefts, rights):
        return project(lefts[0], rights[0]) + project(lefts[1], rights[1])

    def joint_back(grads, weights):
        return back_dot(grads[0], weights[0]) + back_dot(grads[1], weights[1])

    x_one = my_half(hidden) + pair_sum(joint(mix_pair, out_pair))
    n_two = scaled_norm(x_one, norm_gains[1]).astype(jnp.bfloat16)
    caption = image_ids[:, 0, 0]
    chosen = context[caption]
    text_len = chosen.shape[1]
    present = (text_mask[caption] > 0)[:, None, None, :]
    cq_pres, cross_qs, cross_ks, cross_vs, ck_pres, cross_mixes, cross_totals = [], [], [], [], [], [], []
    for group in range(2):
        cq_pre = project(n_two, cq_pair[group]).reshape(half_heads)
        cross_queries = scaled_norm(cq_pre, qk_gains[2]).astype(jnp.bfloat16)
        ckv_pre = jnp.einsum(
            "ptc,sce->spte", chosen, ckv_pair[group], preferred_element_type=jnp.float32
        )
        ckv_pre = ckv_pre.reshape(2, pack_count, text_len, local_heads, head_dim)
        cross_keys = scaled_norm(ckv_pre[0], qk_gains[3]).astype(jnp.bfloat16)
        cross_values = ckv_pre[1].astype(jnp.bfloat16)
        cross_mix, cross_total = forward_attention(cross_queries, cross_keys, cross_values, present)
        cq_pres.append(cq_pre)
        cross_qs.append(cross_queries)
        cross_ks.append(cross_keys)
        cross_vs.append(cross_values)
        ck_pres.append(ckv_pre[0])
        cross_mixes.append(cross_mix.reshape(half_total, head_width))
        cross_totals.append(cross_total)
    x_two = x_one + pair_sum(joint(cross_mixes, cout_pair))
    n_three = scaled_norm(x_two, norm_gains[2]).astype(jnp.bfloat16)
    up_pres = [project(n_three, up_pair[group]) for group in range(2)]
    acts = [jax.nn.gelu(up_pre, approximate=True).astype(jnp.bfloat16) for up_pre in up_pres]
    x_three = x_two + pair_sum(joint(acts, down_pair))
    n_four = norm_rows(x_three).astype(jnp.bfloat16)
    result = project(n_four, final_weight).astype(jnp.bfloat16)
    result = both_halves(result, swapped(result, "zh"))
    grad_final = outer_sum(n_four, grad_result)
    unused, pull = jax.vjp(norm_rows, x_three)
    grad_stream = pull(back_dot(grad_result, final_weight))[0]
    branch = grad_stream.astype(jnp.bfloat16)
    grad_down = outer_sum(branch, jnp.concatenate(acts, 1)).astype(jnp.bfloat16)
    grad_ups = []
    for group in range(2):
        unused, pull = jax.vjp(functools.partial(jax.nn.gelu, approximate=True), up_pres[group])
        grad_ups.append(pull(back_dot(branch, down_pair[group]))[0].astype(jnp.bfloat16))
    grad_up = outer_sum(n_three, jnp.concatenate(grad_ups, 1)).astype(jnp.bfloat16)
    grad_n_three = pair_sum(joint_back(grad_ups, up_pair))
    unused, pull = jax.vjp(scaled_norm, x_two, norm_gains[2])
    grad_input, gain_three = pull(grad_n_three)
    grad_stream = grad_stream + grad_input
    branch = grad_stream.astype(jnp.bfloat16)
    grad_cout = outer_sum(branch, jnp.concatenate(cross_mixes, 1)).astype(jnp.bfloat16)
    gain_cq, gain_ck = 0.0, 0.0
    grad_cqs, grad_cks, grad_cvs = [], [], []
    for group in range(2):
        grad_cmix = back_dot(branch, cout_pair[group]).astype(jnp.bfloat16).reshape(half_heads)
        grad_cq, grad_ck, grad_cv = backward_attention(
            cross_qs[group], cross_ks[group], cross_vs[group], present, cross_totals[group], grad_cmix
        )
        unused, pull = jax.vjp(scaled_norm, cq_pres[group], qk_gains[2])
        grad_cq_pre, gain = pull(grad_cq)
        gain_cq = gain_cq + gain
        unused, pull = jax.vjp(scaled_norm, ck_pres[group], qk_gains[3])
        grad_ck_pre, gain = pull(grad_ck)
        gain_ck = gain_ck + gain
        text_shape = (pack_count, text_len, head_width)
        grad_cqs.append(grad_cq_pre.astype(jnp.bfloat16).reshape(half_total, head_width))
        grad_cks.append(grad_ck_pre.astype(jnp.bfloat16).reshape(text_shape))
        grad_cvs.append(grad_cv.astype(jnp.bfloat16).reshape(text_shape))
    grad_cq_w = outer_sum(n_two, jnp.concatenate(grad_cqs, 1)).astype(jnp.bfloat16)
    grad_ckv_w = jnp.einsum(
        "ptc,pte->ce",
        chosen,
        jnp.concatenate([grad_cks[0], grad_cvs[0], grad_cks[1], grad_cvs[1]], 2),
        preferred_element_type=jnp.float32,
    ).astype(jnp.bfloat16)
    grad_n_two = pair_sum(joint_back(grad_cqs, cq_pair))
    unused, pull = jax.vjp(scaled_norm, x_one, norm_gains[1])
    grad_input, gain_two = pull(grad_n_two)
    grad_stream = grad_stream + grad_input
    branch = grad_stream.astype(jnp.bfloat16)
    grad_out = outer_sum(branch, jnp.concatenate(mix_pair, 1)).astype(jnp.bfloat16)
    grad_amixes = [back_dot(branch, out_pair[group]).astype(jnp.bfloat16) for group in range(2)]
    grad_amix = both_halves(grad_amixes[0], swapped(grad_amixes[1], "zh"))
    head_shape = (pack_count, cells, local_heads, head_dim)
    grad_q, grad_k_near, grad_v_near = backward_attention(
        queries, near_keys, near_values, everywhere, self_total, grad_amix.reshape(head_shape)
    )
    grad_kv = returned(
        jnp.stack([grad_k_near, grad_v_near]).reshape(2, pack_count, 4 * cells, head_width), cells
    )
    grad_kv = grad_kv.reshape(2, pack_count, cells, local_heads, head_dim)
    unused, pull = jax.vjp(turning, projected[0], qk_gains[0])
    grad_q_pre, gain_q = pull(grad_q)
    unused, pull = jax.vjp(turning, projected[1], qk_gains[1])
    grad_k_pre, gain_k = pull(grad_kv[0])
    grad_proj = (
        jnp.stack([grad_q_pre, grad_k_pre, grad_kv[1]])
        .astype(jnp.bfloat16)
        .reshape(3, row_total, head_width)
    )
    grad_qkv = jnp.einsum("rd,sre->dse", n_one, grad_proj, preferred_element_type=jnp.float32)
    grad_qkv = grad_qkv.astype(jnp.bfloat16).reshape(model_width, 3 * head_width)
    grad_n_one = jnp.einsum("sre,sde->rd", grad_proj, qkv_weight, preferred_element_type=jnp.float32)
    fine = grad_n_one.astype(jnp.bfloat16).reshape(pack_count, 2, 2, quarter_cells, model_width)
    kept = pick(fine, lower, 2).astype(jnp.float32)
    kept = kept + swapped(pick(fine, 1 - lower, 2), "zl").astype(jnp.float32)
    sent = swapped(pick(kept, 1 - upper, 1).astype(jnp.bfloat16), "zh").astype(jnp.float32)
    quarter_total = row_total // 4
    grad_n_one = (pick(kept, upper, 1) + sent).reshape(quarter_total, model_width)

    def my_quarter(half_rows):
        cut = pick(half_rows.reshape(pack_count, 2, quarter_cells, model_width), lower, 1)
        return cut.reshape(quarter_total, model_width)

    unused, pull = jax.vjp(scaled_norm, my_quarter(my_half(hidden)), norm_gains[0])
    grad_input, gain_one = pull(grad_n_one)
    branch = (my_quarter(grad_stream) + grad_input).astype(jnp.bfloat16)
    quarter = branch.reshape(pack_count, quarter_cells, model_width)
    facing = swapped(quarter, "zl")
    first = jnp.where(lower == 0, quarter, facing)
    second = jnp.where(lower == 0, facing, quarter)
    half = jnp.stack([first, second], 1).reshape(half_total, model_width)
    branch = both_halves(half, swapped(half, "zh"))
    share = model_width // 4
    my_share = lax.dynamic_slice_in_dim(branch, (2 * upper + lower) * share, share, 1)
    grad_skip_w = outer_sum(normed, my_share).astype(jnp.bfloat16)
    unused, pull = jax.vjp(scaled_norm, joined, skip_gain)
    grad_joined, gain_skip = pull(back_dot(branch, skip_weight))
    grad_skip = grad_joined[:, model_width:].astype(jnp.bfloat16).reshape(skip_in.shape)
    grad_embed = grad_joined[:, :model_width].astype(jnp.bfloat16)
    grad_patch_w = outer_sum(patches, grad_embed)
    grad_patches = back_dot(grad_embed, patch_weight).astype(jnp.bfloat16)
    placed = jnp.concatenate([result, grad_patches], 1)
    placed = placed.reshape(pack_count, tile_side, tile_side, both_channels, 2, 2).transpose(
        0, 3, 1, 4, 2, 5
    )
    placed = placed.reshape(pack_count, both_channels, 2 * tile_side, 2 * tile_side)
    placed = jnp.pad(placed, ((0, 0), (0, 0), (1, 0), (1, 0)))
    moved_cols = from_behind(placed[:, :, :, -1:], ("chi", "clo"), 1)
    placed = jnp.concatenate([moved_cols, placed[:, :, :, 1:-1]], 3)
    moved_rows = from_behind(placed[:, :, -1:, :], ("x", "core"), 1)
    placed = jnp.concatenate([moved_rows, placed[:, :, 1:-1, :]], 2)
    out_latent = placed[:, :out_channels]
    grad_latent = placed[:, out_channels:]
    norm_parts = jnp.stack([gain_one, 0.5 * gain_two, 0.5 * gain_three])
    qk_parts = jnp.stack([gain_q, gain_k, gain_cq, gain_ck])
    gains_total, skip_gain_total, qk_total = lax.psum(
        (norm_parts, 0.25 * gain_skip, qk_parts), EVERYONE
    )

    def scattered(grads):
        return lax.psum_scatter(grads, TILES, scatter_dimension=0, tiled=True)

    def paired(grads):
        mine, other = jnp.split(scattered(grads), 2, 1)
        return mine.astype(jnp.float32) + swapped(other, "zh").astype(jnp.float32)

    sum_down = paired(grad_down).T
    sum_up = paired(grad_up)
    sum_cout = paired(grad_cout).T
    sum_cq = paired(grad_cq_w)
    sum_ckv = paired(grad_ckv_w).reshape(-1, 2, head_width).transpose(1, 0, 2)
    sum_out = paired(grad_out).T
    sum_qkv = scattered(grad_qkv).astype(jnp.float32).reshape(-1, 3, head_width).transpose(1, 0, 2)
    sum_final = scattered(grad_final.astype(jnp.bfloat16))
    sum_final = sum_final.astype(jnp.float32) + swapped(sum_final, "zh").astype(jnp.float32)
    sum_patch = lax.psum_scatter(
        grad_patch_w.astype(jnp.bfloat16), TILES, scatter_dimension=1, tiled=True
    ).astype(jnp.float32)
    sum_skip = lax.all_gather(scattered(grad_skip_w), ("zh", "zl"), axis=1, tiled=True)
    return (
        out_latent,
        grad_latent,
        grad_skip,
        sum_patch,
        skip_gain_total,
        sum_skip.astype(jnp.float32),
        gains_total,
        sum_qkv,
        qk_total,
        sum_out,
        sum_cq,
        sum_ckv,
        sum_cout,
        sum_up,
        sum_down,
        sum_final,
    )


def solution(mesh):
    rows, cols, heads = mesh.devices.shape
    fine = Mesh(
        mesh.devices.reshape(rows // 2, 2, cols // 2, 2, heads // 2, 2),
        ("x", "core", "chi", "clo", "zh", "zl"),
    )
    rows, cols, heads = ("x", "core"), ("chi", "clo"), ("zh", "zl")
    in_specs = (
        P(None, None, rows, cols),
        P(None, rows, cols, None),
        P(),
        P(None, rows, cols),
        P(),
        P(),
        P(),
        P(),
        P(),
        P(None, None, heads),
        P(),
        P(heads, None),
        P(None, heads),
        P(None, None, heads),
        P(heads, None),
        P(None, heads),
        P(heads, None),
        P(),
        P(None, None, rows, cols),
    )
    out_specs = (
        P(None, None, rows, cols),
        P(None, None, rows, cols),
        P(None, rows, cols, None),
        P(None, TILES),
        P(),
        P(TILES, None),
        P(),
        P(None, TILES, heads),
        P(),
        P(heads, TILES),
        P(TILES, heads),
        P(None, TILES, heads),
        P(heads, TILES),
        P(TILES, heads),
        P(heads, TILES),
        P(TILES, None),
    )
    return jax.shard_map(shards, mesh=fine, in_specs=in_specs, out_specs=out_specs, check_vma=False)
```

```python
import functools
import math

import jax
import jax.numpy as jnp
from jax import lax
from jax.experimental import pallas as pl
from jax.experimental.pallas import tpu as pltpu
from jax.sharding import Mesh, PartitionSpec as P

EPSILON = 1e-06


TILES = ("x", "core", "chi", "clo")
SHARERS = ("x", "core", "clo")
EVERYONE = ("x", "core", "chi", "clo", "zh", "zl")


def swapped(value, axis):
    return lax.ppermute(value, axis, [(i, i ^ 1) for i in range(lax.axis_size(axis))])


def from_behind(value, axis, by):
    devices = math.prod(lax.axis_size(name) for name in axis)
    pairs = [(i, i + by) for i in range(devices) if 0 <= i + by < devices]
    return lax.ppermute(value, axis, pairs)


def pick(values, index, axis):
    return lax.dynamic_index_in_dim(values, index, axis, keepdims=False)


def after(value, others):
    return lax.optimization_barrier((value, others))[0]


def sharer_slice(weight):
    sharers = math.prod(lax.axis_size(axis) for axis in SHARERS)
    depth = weight.shape[0] // sharers
    return lax.dynamic_slice_in_dim(weight, lax.axis_index(SHARERS) * depth, depth, 0)


def tile_sums(parts):
    axes = ("x", "core", "chi", "clo")
    sizes = [lax.axis_size(axis) for axis in axes]
    tiles = math.prod(sizes)
    blocks = [part.reshape(*sizes, part.shape[0] // tiles, part.shape[1]) for part in parts]

    def halved(blocks, axis, at):
        here = lax.axis_index(axis)
        sent = jnp.concatenate([pick(block, 1 - here, at) for block in blocks], -2)
        kept = jnp.concatenate([pick(block, here, at) for block in blocks], -2)
        total = kept.astype(jnp.float32) + swapped(sent, axis).astype(jnp.float32)
        return total.astype(jnp.bfloat16)

    total = halved(blocks, "core", 1)
    total = halved([total], "x", 0)
    total = halved([total], "clo", 1)
    if sizes[2] == 1:
        return total[0]
    return lax.psum_scatter(total, "chi", scatter_dimension=0, tiled=False)


def everyones_sum(values):
    for axis in ("core", "x", "clo", "zl", "zh"):
        values = values + swapped(values, axis)
    return values if lax.axis_size("chi") == 1 else lax.psum(values, "chi")


def partner_shard(weight, earlier):
    piece = swapped(sharer_slice(weight), "zh")
    return lax.all_gather(after(piece, earlier), SHARERS, axis=0, tiled=True)


def to_core(value):
    return swapped(value, "core")


def to_side(value):
    return swapped(value, "clo")


def to_corner(value):
    pairs = [(i, 3 - i) for i in range(4)]
    return lax.ppermute(value, ("core", "clo"), pairs)


PARTNERS = (to_core, to_side, to_corner)


def pair_sum(partial, meanwhile=()):
    mine = lax.optimization_barrier(partial.astype(jnp.bfloat16))
    other = after(swapped(mine, "zl"), meanwhile)
    return mine.astype(jnp.float32) + other.astype(jnp.float32)


def norm_rows(values):
    center = values - jnp.mean(values, -1, keepdims=True)
    spread = jnp.mean(center * center, -1, keepdims=True)
    return center * lax.rsqrt(spread + EPSILON)


def scaled_norm(values, gain):
    return norm_rows(values) * gain


def rope_tables(row_pos, col_pos, head_dim):
    quarter = head_dim // 4
    freqs = 10000.0 ** (-jnp.arange(quarter, dtype=jnp.float32) / quarter)
    row_angle = row_pos.astype(jnp.float32)[:, None] * freqs[None, :]
    col_angle = col_pos.astype(jnp.float32)[:, None] * freqs[None, :]
    cosine = jnp.concatenate(
        [jnp.cos(row_angle), jnp.cos(row_angle), jnp.cos(col_angle), jnp.cos(col_angle)], -1
    )
    sine = jnp.concatenate(
        [jnp.sin(row_angle), jnp.sin(row_angle), jnp.sin(col_angle), jnp.sin(col_angle)], -1
    )
    return (cosine, sine)


def project(left, right):
    return jnp.dot(left, right, preferred_element_type=jnp.float32)


def outer_sum(left, right):
    return jnp.einsum("rd,re->de", left, right, preferred_element_type=jnp.float32)


def back_dot(grads, weight):
    return jnp.einsum("re,de->rd", grads, weight, preferred_element_type=jnp.float32)


def float_dot(left, right):
    high = left.astype(jnp.bfloat16)
    low = (left - high.astype(jnp.float32)).astype(jnp.bfloat16)
    total = jnp.dot(high, right, preferred_element_type=jnp.float32)
    return total + jnp.dot(low, right, preferred_element_type=jnp.float32)


def dot_rows(left, right):
    return lax.dot_general(left, right, (((1,), (1,)), ((), ())), preferred_element_type=jnp.float32)


def dot_cols(left, right):
    return lax.dot_general(left, right, (((0,), (0,)), ((), ())), preferred_element_type=jnp.float32)


def head_hat(values, same, head_dim):
    center = values - float_dot(values, same) * (1.0 / head_dim)
    spread = float_dot(center * center, same) * (1.0 / head_dim)
    scale = lax.rsqrt(spread + EPSILON)
    return center * scale, scale


def head_hat_back(hat, scale, grads, same, head_dim):
    mean = float_dot(grads, same) * (1.0 / head_dim)
    along = float_dot(grads * hat, same) * (1.0 / head_dim)
    return scale * (grads - mean - hat * along)


def accumulate(ref, value):
    @pl.when(pl.program_id(0) == 0)
    def _():
        ref[...] = jnp.zeros_like(ref)

    ref[...] += value


def turn_kernel(head_dim, proj, cosine, sine, gains, same, turn, queries, near):
    for part in range(2):
        hat, _ = head_hat(proj[part], same[...], head_dim)
        scaled = hat * gains[part : part + 1]
        turned = scaled * cosine[...] + float_dot(scaled, turn[...]) * sine[...]
        if part == 0:
            queries[0] = turned.astype(queries.dtype)
        else:
            near[0, 0] = turned.astype(near.dtype)
    near[1, 0] = proj[2].astype(near.dtype)


def turn_back_kernel(
    head_dim, proj, grad_q, own, one, two, three, cosine, sine, gains, same, back, grads, gain_sums
):
    sums = []
    for part in range(2):
        if part == 0:
            grad = grad_q[0]
        else:
            grad = own[0, 0] + one[0, 0].astype(jnp.float32)
            grad = grad + two[0, 0].astype(jnp.float32) + three[0, 0].astype(jnp.float32)
        hat, scale = head_hat(proj[part], same[...], head_dim)
        grad = grad * cosine[...] + float_dot(grad * sine[...], back[...])
        sums.append(jnp.sum(grad * hat, 0, keepdims=True))
        grad = head_hat_back(hat, scale, grad * gains[part : part + 1], same[...], head_dim)
        grads[part] = grad.astype(grads.dtype)
    grad = own[1, 0] + one[1, 0].astype(jnp.float32)
    grad = grad + two[1, 0].astype(jnp.float32) + three[1, 0].astype(jnp.float32)
    grads[2] = grad.astype(grads.dtype)
    accumulate(gain_sums, jnp.concatenate(sums + [jnp.zeros((6, sums[0].shape[1]), jnp.float32)], 0))


def attend_kernel(heads, scaling, queries, near_a, near_b, near_c, near_d, masks, mixture, totals):
    nears = (near_a, near_b, near_c, near_d)
    lane = lax.broadcasted_iota(jnp.int32, totals.shape[1:], 1)
    mixed = jnp.zeros(mixture.shape[1:], jnp.float32)
    logs = jnp.zeros(totals.shape[1:], jnp.float32)
    for head in range(heads):
        mask = masks[head : head + 1]
        query = queries[0] * mask
        scores = [dot_rows(query, near[0, 0]) * scaling for near in nears]
        highest = functools.reduce(jnp.maximum, [jnp.max(s, -1, keepdims=True) for s in scores])
        expo = [jnp.exp(s - highest) for s in scores]
        total = functools.reduce(jnp.add, [jnp.sum(e, -1, keepdims=True) for e in expo])
        inverse = 1.0 / total
        for e, near in zip(expo, nears):
            weights = (e * inverse).astype(jnp.bfloat16)
            mixed += jnp.dot(weights, near[1, 0] * mask, preferred_element_type=jnp.float32)
        logs = jnp.where(lane == head, highest + jnp.log(total), logs)
    mixture[0] = mixed.astype(mixture.dtype)
    totals[0] = logs


def attend_back_kernel(
    heads,
    scaling,
    queries,
    near_a,
    near_b,
    near_c,
    near_d,
    masks,
    totals,
    grad_mix,
    grad_q,
    grad_a,
    grad_b,
    grad_c,
    grad_d,
    sums,
):
    nears = (near_a, near_b, near_c, near_d)
    lane = lax.broadcasted_iota(jnp.int32, totals.shape[1:], 1)
    grad_query = jnp.zeros(grad_q.shape[1:], jnp.float32)
    for head in range(heads):
        mask = masks[head : head + 1]
        query = queries[0] * mask
        grad_out = grad_mix[0] * mask
        log_total = jnp.sum(jnp.where(lane == head, totals[0], 0.0), -1, keepdims=True)
        weights = [jnp.exp(dot_rows(query, near[0, 0]) * scaling - log_total) for near in nears]
        grad_w = [dot_rows(grad_out, near[1, 0]) for near in nears]
        inner = functools.reduce(
            jnp.add, [jnp.sum(w * g, -1, keepdims=True) for w, g in zip(weights, grad_w)]
        )
        for at, near in enumerate(nears):
            grad_scores = (weights[at] * (grad_w[at] - inner)).astype(jnp.bfloat16)
            grad_query += jnp.dot(grad_scores, near[0, 0] * mask, preferred_element_type=jnp.float32)
            grad_key = dot_cols(grad_scores, query)
            grad_value = dot_cols(weights[at].astype(jnp.bfloat16), grad_out)
            if head == 0:
                sums[at, 0] = grad_key
                sums[at, 1] = grad_value
            else:
                sums[at, 0] += grad_key
                sums[at, 1] += grad_value
    grad_q[0] = grad_query * scaling
    for at, out in enumerate((grad_a, grad_b, grad_c, grad_d)):
        out[0, 0] = (sums[at, 0] * scaling).astype(out.dtype)
        out[1, 0] = sums[at, 1].astype(out.dtype)


def text_kernel(head_dim, text, gains, same, keys_values):
    for group in range(2):
        hat, _ = head_hat(text[group, 0, 0], same[...], head_dim)
        keys_values[group, 0, 0] = (hat * gains[1:2]).astype(keys_values.dtype)
        keys_values[group, 1, 0] = text[group, 1, 0].astype(keys_values.dtype)


def text_back_kernel(head_dim, text, grads, gains, same, grad_text, gain_sums):
    width = grad_text.shape[4]
    gain_k = jnp.zeros((1, width), jnp.float32)
    for group in range(2):
        hat, scale = head_hat(text[group, 0, 0], same[...], head_dim)
        grad = grads[group, 0, 0]
        gain_k += jnp.sum(grad * hat, 0, keepdims=True)
        grad = head_hat_back(hat, scale, grad * gains[1:2], same[...], head_dim)
        grad_text[group, 0, 0] = grad.astype(grad_text.dtype)
        grad_text[group, 1, 0] = grads[group, 1, 0].astype(grad_text.dtype)
    accumulate(gain_sums, jnp.concatenate([gain_k, jnp.zeros((7, width), jnp.float32)], 0))


def cross_kernel(heads, head_dim, scaling, pre, text, present, gains, same, masks, mixture, totals):
    lane = lax.broadcasted_iota(jnp.int32, totals.shape[2:], 1)
    allowed = present[0] > 0
    for group in range(2):
        hat, _ = head_hat(pre[group, 0], same[...], head_dim)
        queries = (hat * gains[0:1]).astype(jnp.bfloat16)
        keys, values = text[group, 0, 0], text[group, 1, 0]
        mixed = jnp.zeros(mixture.shape[2:], jnp.float32)
        logs = jnp.zeros(totals.shape[2:], jnp.float32)
        for head in range(heads):
            mask = masks[head : head + 1]
            scores = jnp.where(allowed, dot_rows(queries * mask, keys) * scaling, -1e30)
            highest = jnp.max(scores, -1, keepdims=True)
            expo = jnp.exp(scores - highest)
            total = jnp.sum(expo, -1, keepdims=True)
            weights = (expo * (1.0 / total)).astype(jnp.bfloat16)
            mixed += jnp.dot(weights, values * mask, preferred_element_type=jnp.float32)
            logs = jnp.where(lane == head, highest + jnp.log(total), logs)
        mixture[group, 0] = mixed.astype(mixture.dtype)
        totals[group, 0] = logs


def cross_back_kernel(
    heads,
    head_dim,
    scaling,
    pre,
    text,
    present,
    gains,
    same,
    masks,
    totals,
    grad_mix,
    grad_pre,
    grad_text,
    gain_sums,
):
    lane = lax.broadcasted_iota(jnp.int32, totals.shape[2:], 1)
    allowed = present[0] > 0
    width = grad_pre.shape[3]
    gain_q = jnp.zeros((1, width), jnp.float32)
    for group in range(2):
        q_hat, q_scale = head_hat(pre[group, 0], same[...], head_dim)
        queries = (q_hat * gains[0:1]).astype(jnp.bfloat16)
        keys, values = text[group, 0, 0], text[group, 1, 0]
        grad_q = jnp.zeros(grad_pre.shape[2:], jnp.float32)
        for head in range(heads):
            mask = masks[head : head + 1]
            query = queries * mask
            grad_out = grad_mix[group, 0] * mask
            log_total = jnp.sum(jnp.where(lane == head, totals[group, 0], 0.0), -1, keepdims=True)
            scores = jnp.where(allowed, dot_rows(query, keys) * scaling, -1e30)
            weights = jnp.exp(scores - log_total)
            grad_w = dot_rows(grad_out, values)
            inner = jnp.sum(weights * grad_w, -1, keepdims=True)
            grad_scores = (weights * (grad_w - inner)).astype(jnp.bfloat16)
            grad_q += jnp.dot(grad_scores, keys * mask, preferred_element_type=jnp.float32)
            grad_k = dot_cols(grad_scores, query) * scaling
            grad_v = dot_cols(weights.astype(jnp.bfloat16), grad_out)
            if head == 0:
                grad_text[group, 0, 0] = grad_k
                grad_text[group, 1, 0] = grad_v
            else:
                grad_text[group, 0, 0] += grad_k
                grad_text[group, 1, 0] += grad_v
        grad_q = grad_q * scaling
        gain_q += jnp.sum(grad_q * q_hat, 0, keepdims=True)
        grad_q = head_hat_back(q_hat, q_scale, grad_q * gains[0:1], same[...], head_dim)
        grad_pre[group, 0] = grad_q.astype(grad_pre.dtype)
    accumulate(gain_sums, jnp.concatenate([gain_q, jnp.zeros((7, width), jnp.float32)], 0))


def whole(array):
    rank = len(array.shape)
    return pl.BlockSpec(array.shape, lambda pack: (0,) * rank)


def by_pack(array, axis, depth=1):
    shape = array.shape[:axis] + (depth,) + array.shape[axis + 1 :]
    rank = len(shape)
    return pl.BlockSpec(shape, lambda pack: tuple(pack if at == axis else 0 for at in range(rank)))


def per_pack(body, packs, inputs, outputs, flops, scratch=()):
    ins, in_specs, out_specs, shapes = [], [], [], []
    for array, axis, depth in inputs:
        ins.append(array)
        in_specs.append(whole(array) if axis is None else by_pack(array, axis, depth))
    for shape, dtype, axis, depth in outputs:
        spec = jax.ShapeDtypeStruct(shape, dtype)
        shapes.append(spec)
        out_specs.append(whole(spec) if axis is None else by_pack(spec, axis, depth))
    moved = sum(math.prod(a.shape) * a.dtype.itemsize for a in ins + shapes)
    return pl.pallas_call(
        body,
        grid=(packs,),
        in_specs=in_specs,
        out_specs=out_specs,
        out_shape=shapes,
        scratch_shapes=scratch,
        cost_estimate=pl.CostEstimate(flops=flops, bytes_accessed=moved, transcendentals=0),
        compiler_params=pltpu.CompilerParams(
            dimension_semantics=("arbitrary",), vmem_limit_bytes=48 * 1024 * 1024
        ),
    )(*ins)


def shards(
    latent,
    skip_in,
    context,
    image_ids,
    text_mask,
    patch_weight,
    skip_gain,
    skip_weight,
    norm_gains,
    qkv_weight,
    qk_gains,
    out_weight,
    cq_weight,
    ckv_weight,
    cout_weight,
    up_weight,
    down_weight,
    final_weight,
    cotangent,
):
    pack_count = latent.shape[0]
    in_channels = latent.shape[1]
    out_channels = cotangent.shape[1]
    tile_side = image_ids.shape[1]
    cells = tile_side * tile_side
    row_total = pack_count * cells
    model_width = skip_weight.shape[1]
    head_dim = qk_gains.shape[1]
    true_width = qkv_weight.shape[2]
    local_heads = true_width // head_dim
    head_width = -(-true_width // 128) * 128
    spare = head_width - true_width
    both_channels = in_channels + out_channels
    half_cells = cells // 2
    quarter_cells = cells // 4
    half_total = row_total // 2
    quarter_total = row_total // 4
    text_width = context.shape[2]
    tiles = math.prod(lax.axis_size(axis) for axis in TILES)
    upper, lower = lax.axis_index("zh"), lax.axis_index("zl")
    scaling = 1.0 / math.sqrt(head_dim)
    bf16 = jnp.bfloat16

    def my_half(values):
        shape = values.shape[1:]
        cut = pick(values.reshape(pack_count, 2, half_cells, *shape), upper, 1)
        return cut.reshape(half_total, *shape)

    def other_half(values):
        shape = values.shape[1:]
        cut = pick(values.reshape(pack_count, 2, half_cells, *shape), 1 - upper, 1)
        return cut.reshape(half_total, *shape)

    def both_halves(mine, other):
        shape = mine.shape[1:]
        mine = mine.reshape(pack_count, half_cells, *shape)
        other = other.reshape(pack_count, half_cells, *shape)
        first = jnp.where(upper == 0, mine, other)
        second = jnp.where(upper == 0, other, mine)
        return jnp.stack([first, second], 1).reshape(row_total, *shape)

    stacked = jnp.concatenate([latent, cotangent], 1)
    lower_rim = from_behind(stacked[:, :, :1, :], ("x", "core"), -1)
    stacked = jnp.concatenate([stacked, lower_rim], 2)
    right_rim = from_behind(stacked[:, :, :, :1], ("chi", "clo"), -1)
    stacked = jnp.concatenate([stacked, right_rim], 3)[:, :, 1:, 1:]
    pieces = stacked.reshape(pack_count, both_channels, tile_side, 2, tile_side, 2)
    pieces = pieces.transpose(0, 2, 4, 1, 3, 5).reshape(row_total, both_channels * 4)
    patches = pieces[:, : in_channels * 4]
    grad_result = my_half(pieces[:, in_channels * 4 :])

    def spread_heads(values):
        return jnp.pad(jnp.tile(values, (1, local_heads)), ((0, 0), (0, spare)))

    qkv_wide = jnp.pad(qkv_weight, ((0, 0), (0, 0), (0, spare)))
    ckv_wide = jnp.pad(ckv_weight, ((0, 0), (0, 0), (0, spare)))
    out_tall, cout_tall, cq_tall = [
        jnp.pad(weight, ((0, spare), (0, 0))) for weight in (out_weight, cout_weight, cq_weight.T)
    ]
    token_index = jnp.arange(cells, dtype=jnp.int32)
    row_pos = lax.axis_index("core") * tile_side + token_index // tile_side
    col_pos = lax.axis_index("clo") * tile_side + token_index % tile_side
    cosine, sine = rope_tables(row_pos, col_pos, head_dim)
    cosine, sine = spread_heads(cosine), spread_heads(sine)
    lanes = jnp.arange(head_width, dtype=jnp.int32)
    head_of, place = lanes // head_dim, lanes % head_dim
    same = (head_of[:, None] == head_of[None, :]).astype(bf16)
    quarter = head_dim // 4
    ahead = (place // quarter % 2 == 0)[None, :]
    turn = jnp.where(
        ahead,
        -(lanes[:, None] == lanes[None, :] + quarter).astype(bf16),
        (lanes[:, None] == lanes[None, :] - quarter).astype(bf16),
    )
    masks = (jnp.arange(8, dtype=jnp.int32)[:, None] == head_of[None, :]).astype(bf16)
    flat_gains = spread_heads(jnp.pad(qk_gains, ((0, 4), (0, 0))))
    self_gains, cross_gains = flat_gains, jnp.roll(flat_gains, -2, 0)

    embed = project(patches, patch_weight)
    joined = jnp.concatenate(
        [embed, skip_in.reshape(row_total, model_width).astype(jnp.float32)], 1
    )
    normed = scaled_norm(joined, skip_gain).astype(bf16)
    slices = [sharer_slice(weight) for weight in (out_tall, cout_tall, cq_tall)]
    moved = swapped(jnp.stack(slices), "zh")
    gathered = lax.all_gather(after(moved, normed), SHARERS, axis=0, tiled=False)
    out_other, cout_other, cq_other = [
        gathered[:, at].reshape(head_width, model_width) for at in range(3)
    ]
    hidden = project(normed, skip_weight)
    ckv_other = partner_shard(ckv_wide.reshape(2 * text_width, head_width), hidden)
    out_pair = (out_tall, out_other)
    cq_pair = (cq_tall, cq_other)
    ckv_pair = (ckv_wide, ckv_other.reshape(ckv_wide.shape))
    cout_pair = (cout_tall, cout_other)
    n_one = scaled_norm(hidden, norm_gains[0]).astype(bf16)
    projected = jnp.einsum("rd,sde->sre", n_one, qkv_wide, preferred_element_type=jnp.float32)
    tile_flat = (pack_count, cells, head_width)
    near_flat = (2, pack_count, cells, head_width)
    queries, near_own = per_pack(
        functools.partial(turn_kernel, head_dim),
        pack_count,
        [
            (projected, 1, cells),
            (cosine, None, 1),
            (sine, None, 1),
            (self_gains, None, 1),
            (same, None, 1),
            (turn, None, 1),
        ],
        [(tile_flat, bf16, 0, 1), (near_flat, bf16, 1, 1)],
        row_total * head_width * head_width * 36,
    )
    up_both = jnp.concatenate([up_weight, partner_shard(up_weight, near_own)], 1)
    down_both = jnp.concatenate([down_weight, partner_shard(down_weight, near_own)], 0)
    nears = (near_own,) + tuple(to_partners(near_own) for to_partners in PARTNERS)
    near_args = [(near, 1, 1) for near in nears]
    self_flops = row_total * 4 * cells * head_width * local_heads * 4
    mixture, self_totals = per_pack(
        functools.partial(attend_kernel, local_heads, scaling),
        pack_count,
        [(queries, 0, 1), *near_args, (masks, None, 1)],
        [(tile_flat, bf16, 0, 1), ((pack_count, cells, 128), jnp.float32, 0, 1)],
        self_flops,
    )
    mixture = mixture.reshape(row_total, head_width)
    mix_pair = (my_half(mixture), swapped(other_half(mixture), "zh"))

    def joint(lefts, rights):
        return project(lefts[0], rights[0]) + project(lefts[1], rights[1])

    def joint_back(grads, weights):
        return back_dot(grads[0], weights[0]) + back_dot(grads[1], weights[1])

    x_one = my_half(hidden) + pair_sum(joint(mix_pair, out_pair))
    n_two = scaled_norm(x_one, norm_gains[1]).astype(bf16)
    caption = after(image_ids[:, 0, 0], near_own)
    text_len = context.shape[1]
    padding = -text_len % 128
    padded_len = text_len + padding
    chosen = jnp.pad(context[caption], ((0, 0), (0, padding), (0, 0)))
    present = jnp.pad((text_mask[caption] > 0).astype(jnp.float32), ((0, 0), (0, padding)))
    present = present[:, None, :]
    text_pre = jnp.stack(
        [
            jnp.einsum("ptc,sce->spte", chosen, weight, preferred_element_type=jnp.float32)
            for weight in ckv_pair
        ]
    )
    cross_pre = jnp.stack([back_dot(n_two, weight) for weight in cq_pair])
    cross_pre = cross_pre.reshape(2, pack_count, half_cells, head_width)
    (text_near,) = per_pack(
        functools.partial(text_kernel, head_dim),
        pack_count,
        [(text_pre, 2, 1), (cross_gains, None, 1), (same, None, 1)],
        [(text_pre.shape, bf16, 2, 1)],
        text_pre.size * head_width * 4,
    )
    cross_args = [
        (cross_pre, 1, 1),
        (text_near, 2, 1),
        (present, 0, 1),
        (cross_gains, None, 1),
        (same, None, 1),
        (masks, None, 1),
    ]
    cross_flat = (2, pack_count, half_cells, head_width)
    cross_flops = half_total * padded_len * head_width * local_heads * 8
    cross_mix, cross_totals = per_pack(
        functools.partial(cross_kernel, local_heads, head_dim, scaling),
        pack_count,
        cross_args,
        [(cross_flat, bf16, 1, 1), ((2, pack_count, half_cells, 128), jnp.float32, 1, 1)],
        cross_flops,
    )
    cross_mixes = [cross_mix[group].reshape(half_total, head_width) for group in range(2)]
    x_two = x_one + pair_sum(joint(cross_mixes, cout_pair))
    n_three = scaled_norm(x_two, norm_gains[2]).astype(bf16)
    up_pre = project(n_three, up_both)
    act = jax.nn.gelu(up_pre, approximate=True).astype(bf16)
    x_three = x_two + pair_sum(project(act, down_both))
    n_four = norm_rows(x_three).astype(bf16)
    result = project(n_four, final_weight).astype(bf16)
    result = both_halves(result, swapped(result, "zh"))
    grad_final = outer_sum(n_four, grad_result)
    unused, pull = jax.vjp(norm_rows, x_three)
    grad_stream = pull(back_dot(grad_result, final_weight))[0]
    branch = grad_stream.astype(bf16)
    unused, pull = jax.vjp(functools.partial(jax.nn.gelu, approximate=True), up_pre)
    grad_up_pre = pull(back_dot(branch, down_both))[0].astype(bf16)
    grad_down = outer_sum(branch, act).astype(bf16)
    grad_up = outer_sum(n_three, grad_up_pre).astype(bf16)
    grad_n_three = pair_sum(back_dot(grad_up_pre, up_both), (grad_down, grad_up))

    def scattered(grads):
        return lax.psum_scatter(grads, TILES, scatter_dimension=0, tiled=True)

    mlp_shares = (scattered(grad_down), scattered(grad_up))
    unused, pull = jax.vjp(scaled_norm, x_two, norm_gains[2])
    grad_input, gain_three = pull(grad_n_three)
    grad_stream = grad_stream + grad_input
    branch = grad_stream.astype(bf16)
    grad_cmix = jnp.stack([back_dot(branch, weight).astype(bf16) for weight in cout_pair])
    grad_cq, grad_text, cross_sums = per_pack(
        functools.partial(cross_back_kernel, local_heads, head_dim, scaling),
        pack_count,
        [*cross_args, (cross_totals, 1, 1), (grad_cmix.reshape(cross_flat), 1, 1)],
        [
            (cross_flat, bf16, 1, 1),
            (text_pre.shape, jnp.float32, 2, 1),
            ((8, head_width), jnp.float32, None, 1),
        ],
        3 * cross_flops,
    )
    grad_cqs = [grad_cq[group].reshape(half_total, head_width) for group in range(2)]
    grad_couts = [outer_sum(branch, mix).astype(bf16) for mix in cross_mixes]
    grad_cq_ws = [outer_sum(n_two, grad).astype(bf16) for grad in grad_cqs]
    grad_n_two = pair_sum(
        project(grad_cqs[0], cq_pair[0]) + project(grad_cqs[1], cq_pair[1]),
        (grad_couts, grad_cq_ws),
    )
    grad_text, text_sums = per_pack(
        functools.partial(text_back_kernel, head_dim),
        pack_count,
        [(text_pre, 2, 1), (grad_text, 2, 1), (cross_gains, None, 1), (same, None, 1)],
        [(text_pre.shape, bf16, 2, 1), ((8, head_width), jnp.float32, None, 1)],
        text_pre.size * head_width * 8,
    )
    grad_ckvs = [
        jnp.einsum(
            "ptc,pte->ce", chosen, grad_text[group, side], preferred_element_type=jnp.float32
        ).astype(bf16)
        for group in range(2)
        for side in range(2)
    ]
    narrow = grad_final.astype(bf16).reshape(tiles, -1, 4 * out_channels).transpose(0, 2, 1)
    narrow = jnp.pad(narrow, ((0, 0), (0, 0), (0, head_width - narrow.shape[2])))
    narrow = narrow.reshape(-1, head_width)
    mine = [grad_couts[0], grad_cq_ws[0], grad_ckvs[0], grad_ckvs[1]]
    other = [grad_couts[1], grad_cq_ws[1], grad_ckvs[2], grad_ckvs[3]]
    cross_shares = (tile_sums(mine + [narrow]), tile_sums(other + [narrow]))
    unused, pull = jax.vjp(scaled_norm, x_one, norm_gains[1])
    grad_input, gain_two = pull(grad_n_two)
    grad_stream = grad_stream + grad_input
    branch = grad_stream.astype(bf16)
    grad_amixes = [back_dot(branch, weight).astype(bf16) for weight in out_pair]
    grad_amix = both_halves(grad_amixes[0], swapped(grad_amixes[1], "zh"))
    grad_outs = [outer_sum(branch, mix).astype(bf16) for mix in mix_pair]
    grad_q, *grad_nears = per_pack(
        functools.partial(attend_back_kernel, local_heads, scaling),
        pack_count,
        [
            (queries, 0, 1),
            *near_args,
            (masks, None, 1),
            (self_totals, 0, 1),
            (grad_amix.reshape(tile_flat), 0, 1),
        ],
        [(tile_flat, jnp.float32, 0, 1), (near_flat, jnp.float32, 1, 1)]
        + [(near_flat, bf16, 1, 1)] * 3,
        self_flops * 5 // 2,
        [pltpu.VMEM((4, 2, cells, head_width), jnp.float32)],
    )
    arrived = [to_partners(grad) for to_partners, grad in zip(PARTNERS, grad_nears[1:])]
    arrived = after(arrived, (mlp_shares, grad_outs))
    grad_proj, self_sums = per_pack(
        functools.partial(turn_back_kernel, head_dim),
        pack_count,
        [
            (projected, 1, cells),
            (grad_q, 0, 1),
            (grad_nears[0], 1, 1),
            *[(grad, 1, 1) for grad in arrived],
            (cosine, None, 1),
            (sine, None, 1),
            (self_gains, None, 1),
            (same, None, 1),
            (turn.T, None, 1),
        ],
        [(projected.shape, bf16, 1, cells), ((8, head_width), jnp.float32, None, 1)],
        row_total * head_width * head_width * 60,
    )
    grad_n_one = jnp.einsum("sre,sde->rd", grad_proj, qkv_wide, preferred_element_type=jnp.float32)
    grad_qkvs = [outer_sum(n_one, grad_proj[part]).astype(bf16) for part in range(3)]
    self_shares = tile_sums(grad_outs + grad_qkvs)
    fine = grad_n_one.astype(bf16).reshape(pack_count, 2, 2, quarter_cells, model_width)
    kept = pick(fine, lower, 2).astype(jnp.float32)
    facing = after(swapped(pick(fine, 1 - lower, 2), "zl"), grad_qkvs)
    kept = kept + facing.astype(jnp.float32)
    sent = swapped(pick(kept, 1 - upper, 1).astype(bf16), "zh").astype(jnp.float32)
    grad_n_one = (pick(kept, upper, 1) + sent).reshape(quarter_total, model_width)

    def my_quarter(half_rows):
        cut = pick(half_rows.reshape(pack_count, 2, quarter_cells, model_width), lower, 1)
        return cut.reshape(quarter_total, model_width)

    unused, pull = jax.vjp(scaled_norm, my_quarter(my_half(hidden)), norm_gains[0])
    grad_input, gain_one = pull(grad_n_one)
    branch = (my_quarter(grad_stream) + grad_input).astype(bf16)
    quarter = branch.reshape(pack_count, quarter_cells, model_width)
    facing = swapped(quarter, "zl")
    first = jnp.where(lower == 0, quarter, facing)
    second = jnp.where(lower == 0, facing, quarter)
    half = jnp.stack([first, second], 1).reshape(half_total, model_width)
    branch = both_halves(half, after(swapped(half, "zh"), (cross_shares, self_shares)))

    def with_partner(mine, other):
        other = swapped(after(other, branch), "zh")
        return mine.astype(jnp.float32) + other.astype(jnp.float32)

    tile_rows = model_width // tiles
    down_mine, down_other = jnp.split(mlp_shares[0], 2, 1)
    up_mine, up_other = jnp.split(mlp_shares[1], 2, 1)
    sum_down = with_partner(down_mine, down_other).T
    sum_up = with_partner(up_mine, up_other)
    cross_total = with_partner(*cross_shares)
    sum_cout = cross_total[:tile_rows, :true_width].T
    sum_cq = cross_total[tile_rows : 2 * tile_rows, :true_width]
    sum_final = cross_total[-4 * out_channels :, :tile_rows].T
    sum_ckv = cross_total[2 * tile_rows : -4 * out_channels, :true_width].reshape(
        2, -1, true_width
    )
    sum_out = with_partner(self_shares[:tile_rows], self_shares[tile_rows : 2 * tile_rows])
    sum_out = sum_out[:, :true_width].T
    sum_qkv = self_shares[2 * tile_rows :, :true_width].astype(jnp.float32)
    sum_qkv = sum_qkv.reshape(3, tile_rows, true_width)
    share_at = (2 * upper + lower) * true_width
    my_share = lax.dynamic_slice_in_dim(branch, share_at, true_width, 1)
    my_share = jnp.pad(my_share, ((0, 0), (0, spare)))
    skip_shares = tile_sums([outer_sum(normed, my_share).astype(bf16)])
    unused, pull = jax.vjp(scaled_norm, joined, skip_gain)
    grad_joined, gain_skip = pull(back_dot(branch, skip_weight))
    grad_skip = grad_joined[:, model_width:].astype(bf16).reshape(skip_in.shape)
    grad_embed = grad_joined[:, :model_width].astype(bf16)
    grad_patch_w = outer_sum(grad_embed, patches)
    grad_patches = back_dot(grad_embed, patch_weight).astype(bf16)
    placed = jnp.concatenate([result, grad_patches], 1)
    placed = placed.reshape(pack_count, tile_side, tile_side, both_channels, 2, 2).transpose(
        0, 3, 1, 4, 2, 5
    )
    placed = placed.reshape(pack_count, both_channels, 2 * tile_side, 2 * tile_side)
    placed = jnp.pad(placed, ((0, 0), (0, 0), (1, 0), (1, 0)))
    moved_cols = from_behind(placed[:, :, :, -1:], ("chi", "clo"), 1)
    placed = jnp.concatenate([moved_cols, placed[:, :, :, 1:-1]], 3)
    moved_rows = from_behind(placed[:, :, -1:, :], ("x", "core"), 1)
    placed = jnp.concatenate([moved_rows, placed[:, :, 1:-1, :]], 2)
    out_latent = placed[:, :out_channels]
    grad_latent = placed[:, out_channels:]
    qk_parts = jnp.concatenate([self_sums[:2], cross_sums[:1], text_sums[:1]], 0)
    qk_parts = jnp.sum(qk_parts[:, :true_width].reshape(4, local_heads, head_dim), 1).reshape(-1)
    gains = [gain_one, 0.5 * gain_two, 0.5 * gain_three, 0.25 * gain_skip[:model_width]]
    gains = gains + [
        0.25 * gain_skip[model_width:],
        jnp.pad(qk_parts, (0, model_width - qk_parts.shape[0])),
    ]
    gains = everyones_sum(jnp.stack(gains))
    gains_total = gains[:3]
    skip_gain_total = gains[3:5].reshape(-1)
    qk_total = gains[5, : 4 * head_dim].reshape(4, head_dim)
    sum_skip = lax.all_gather(skip_shares, ("zh", "zl"), axis=0, tiled=False)
    sum_skip = sum_skip[:, :, :true_width].transpose(1, 0, 2).reshape(-1, model_width)
    sum_patch = tile_sums([grad_patch_w.astype(bf16)]).astype(jnp.float32).T
    return (
        out_latent,
        grad_latent,
        grad_skip,
        sum_patch,
        skip_gain_total,
        sum_skip.astype(jnp.float32),
        gains_total,
        sum_qkv,
        qk_total,
        sum_out,
        sum_cq,
        sum_ckv,
        sum_cout,
        sum_up,
        sum_down,
        sum_final,
    )


def solution(mesh):
    rows, cols, heads = mesh.devices.shape
    fine = Mesh(
        mesh.devices.reshape(rows // 2, 2, cols // 2, 2, heads // 2, 2),
        ("x", "core", "chi", "clo", "zh", "zl"),
    )
    rows, cols, heads = ("x", "core"), ("chi", "clo"), ("zh", "zl")
    in_specs = (
        P(None, None, rows, cols),
        P(None, rows, cols, None),
        P(),
        P(None, rows, cols),
        P(),
        P(),
        P(),
        P(),
        P(),
        P(None, None, heads),
        P(),
        P(heads, None),
        P(None, heads),
        P(None, None, heads),
        P(heads, None),
        P(None, heads),
        P(heads, None),
        P(),
        P(None, None, rows, cols),
    )
    out_specs = (
        P(None, None, rows, cols),
        P(None, None, rows, cols),
        P(None, rows, cols, None),
        P(None, TILES),
        P(),
        P(TILES, None),
        P(),
        P(None, TILES, heads),
        P(),
        P(heads, TILES),
        P(TILES, heads),
        P(None, TILES, heads),
        P(heads, TILES),
        P(TILES, heads),
        P(heads, TILES),
        P(TILES, None),
    )
    return jax.shard_map(shards, mesh=fine, in_specs=in_specs, out_specs=out_specs, check_vma=False)
```

```python
import functools
import math

import jax
import jax.numpy as jnp
from jax import lax
from jax.experimental import pallas as pl
from jax.experimental.pallas import tpu as pltpu
from jax.sharding import Mesh, PartitionSpec as P

EPSILON = 1e-06


TILES = ("x", "core", "chi", "clo")
SHARERS = ("x", "core", "clo")
EVERYONE = ("x", "core", "chi", "clo", "zh", "zl")


def swapped(value, axis):
    return lax.ppermute(value, axis, [(i, i ^ 1) for i in range(lax.axis_size(axis))])


def from_behind(value, axis, by):
    devices = math.prod(lax.axis_size(name) for name in axis)
    pairs = [(i, i + by) for i in range(devices) if 0 <= i + by < devices]
    return lax.ppermute(value, axis, pairs)


def pick(values, index, axis):
    return lax.dynamic_index_in_dim(values, index, axis, keepdims=False)


def after(value, others):
    return lax.optimization_barrier((value, others))[0]


def sharer_slice(weight):
    sharers = math.prod(lax.axis_size(axis) for axis in SHARERS)
    depth = weight.shape[0] // sharers
    return lax.dynamic_slice_in_dim(weight, lax.axis_index(SHARERS) * depth, depth, 0)


def tile_sums(parts):
    axes = ("x", "core", "chi", "clo")
    sizes = [lax.axis_size(axis) for axis in axes]
    tiles = math.prod(sizes)
    blocks = [part.reshape(*sizes, part.shape[0] // tiles, part.shape[1]) for part in parts]

    def halved(blocks, axis, at):
        here = lax.axis_index(axis)
        sent = jnp.concatenate([pick(block, 1 - here, at) for block in blocks], -2)
        kept = jnp.concatenate([pick(block, here, at) for block in blocks], -2)
        total = kept.astype(jnp.float32) + swapped(sent, axis).astype(jnp.float32)
        return lax.reduce_precision(total, 8, 7).astype(jnp.bfloat16)

    by_core = halved(blocks, "core", 1)
    by_x = halved([by_core], "x", 0)
    by_cols = halved([by_x], "clo", 1)
    if sizes[2] == 1:
        return by_core, by_x, by_cols[0]
    return by_core, by_x, lax.psum_scatter(by_cols, "chi", scatter_dimension=0, tiled=False)


def everyones_sum(values):
    for axis in ("core", "x", "clo", "zl", "zh"):
        values = values + swapped(values, axis)
    return values if lax.axis_size("chi") == 1 else lax.psum(values, "chi")


def from_corner(value):
    sizes = [lax.axis_size(axis) for axis in ("x", "core", "chi", "clo")]
    rows, cols = sizes[0] * sizes[1], sizes[2] * sizes[3]
    pairs = [
        ((i + 1) * cols + j + 1, i * cols + j) for i in range(rows - 1) for j in range(cols - 1)
    ]
    return lax.ppermute(value, ("x", "core", "chi", "clo"), pairs)


def partner_shard(weight, earlier):
    piece = swapped(sharer_slice(weight), "zh")
    return lax.all_gather(after(piece, earlier), SHARERS, axis=0, tiled=True)


def to_core(value):
    return swapped(value, "core")


def to_side(value):
    return swapped(value, "clo")


def to_corner(value):
    pairs = [(i, 3 - i) for i in range(4)]
    return lax.ppermute(value, ("core", "clo"), pairs)


PARTNERS = (to_core, to_side, to_corner)


def pair_sum(partial, meanwhile=()):
    mine = lax.optimization_barrier(partial.astype(jnp.bfloat16))
    other = after(swapped(mine, "zl"), meanwhile)
    return mine.astype(jnp.float32) + other.astype(jnp.float32)


def norm_rows(values):
    center = values - jnp.mean(values, -1, keepdims=True)
    spread = jnp.mean(center * center, -1, keepdims=True)
    return center * lax.rsqrt(spread + EPSILON)


def scaled_norm(values, gain):
    return norm_rows(values) * gain


def rope_tables(row_pos, col_pos, head_dim):
    quarter = head_dim // 4
    freqs = 10000.0 ** (-jnp.arange(quarter, dtype=jnp.float32) / quarter)
    row_angle = row_pos.astype(jnp.float32)[:, None] * freqs[None, :]
    col_angle = col_pos.astype(jnp.float32)[:, None] * freqs[None, :]
    cosine = jnp.concatenate(
        [jnp.cos(row_angle), jnp.cos(row_angle), jnp.cos(col_angle), jnp.cos(col_angle)], -1
    )
    sine = jnp.concatenate(
        [jnp.sin(row_angle), jnp.sin(row_angle), jnp.sin(col_angle), jnp.sin(col_angle)], -1
    )
    return (cosine, sine)


def project(left, right):
    return jnp.dot(left, right, preferred_element_type=jnp.float32)


def outer_sum(left, right):
    return jnp.einsum("rd,re->de", left, right, preferred_element_type=jnp.float32)


def back_dot(grads, weight):
    return jnp.einsum("re,de->rd", grads, weight, preferred_element_type=jnp.float32)


def float_dot(left, right):
    high = left.astype(jnp.bfloat16)
    low = (left - high.astype(jnp.float32)).astype(jnp.bfloat16)
    total = jnp.dot(high, right, preferred_element_type=jnp.float32)
    return total + jnp.dot(low, right, preferred_element_type=jnp.float32)


def dot_rows(left, right):
    return lax.dot_general(left, right, (((1,), (1,)), ((), ())), preferred_element_type=jnp.float32)


def dot_cols(left, right):
    return lax.dot_general(left, right, (((0,), (0,)), ((), ())), preferred_element_type=jnp.float32)


def head_hat(values, same, head_dim):
    center = values - float_dot(values, same) * (1.0 / head_dim)
    spread = float_dot(center * center, same) * (1.0 / head_dim)
    scale = lax.rsqrt(spread + EPSILON)
    return center * scale, scale


def head_hat_back(hat, scale, grads, same, head_dim):
    mean = float_dot(grads, same) * (1.0 / head_dim)
    along = float_dot(grads * hat, same) * (1.0 / head_dim)
    return scale * (grads - mean - hat * along)


def accumulate(ref, value):
    @pl.when(pl.program_id(0) == 0)
    def _():
        ref[...] = jnp.zeros_like(ref)

    ref[...] += value


def turn_kernel(head_dim, proj, cosine, sine, gains, same, turn, queries, near):
    for part in range(2):
        hat, _ = head_hat(proj[part], same[...], head_dim)
        scaled = hat * gains[part : part + 1]
        turned = scaled * cosine[...] + float_dot(scaled, turn[...]) * sine[...]
        if part == 0:
            queries[0] = turned.astype(queries.dtype)
        else:
            near[0, 0] = turned.astype(near.dtype)
    near[1, 0] = proj[2].astype(near.dtype)


def turn_back_kernel(
    head_dim, proj, grad_q, own, one, two, three, cosine, sine, gains, same, back, grads, gain_sums
):
    sums = []
    for part in range(2):
        if part == 0:
            grad = grad_q[0]
        else:
            grad = own[0, 0] + one[0, 0].astype(jnp.float32)
            grad = grad + two[0, 0].astype(jnp.float32) + three[0, 0].astype(jnp.float32)
        hat, scale = head_hat(proj[part], same[...], head_dim)
        grad = grad * cosine[...] + float_dot(grad * sine[...], back[...])
        sums.append(jnp.sum(grad * hat, 0, keepdims=True))
        grad = head_hat_back(hat, scale, grad * gains[part : part + 1], same[...], head_dim)
        grads[part] = grad.astype(grads.dtype)
    grad = own[1, 0] + one[1, 0].astype(jnp.float32)
    grad = grad + two[1, 0].astype(jnp.float32) + three[1, 0].astype(jnp.float32)
    grads[2] = grad.astype(grads.dtype)
    accumulate(gain_sums, jnp.concatenate(sums + [jnp.zeros((6, sums[0].shape[1]), jnp.float32)], 0))


def attend_kernel(heads, scaling, queries, near_a, near_b, near_c, near_d, masks, mixture, totals):
    nears = (near_a, near_b, near_c, near_d)
    lane = lax.broadcasted_iota(jnp.int32, totals.shape[1:], 1)
    mixed = jnp.zeros(mixture.shape[1:], jnp.float32)
    logs = jnp.zeros(totals.shape[1:], jnp.float32)
    for head in range(heads):
        mask = masks[head : head + 1]
        query = queries[0] * mask
        scores = [dot_rows(query, near[0, 0]) * scaling for near in nears]
        highest = functools.reduce(jnp.maximum, [jnp.max(s, -1, keepdims=True) for s in scores])
        expo = [jnp.exp(s - highest) for s in scores]
        total = functools.reduce(jnp.add, [jnp.sum(e, -1, keepdims=True) for e in expo])
        inverse = 1.0 / total
        for e, near in zip(expo, nears):
            weights = (e * inverse).astype(jnp.bfloat16)
            mixed += jnp.dot(weights, near[1, 0] * mask, preferred_element_type=jnp.float32)
        logs = jnp.where(lane == head, highest + jnp.log(total), logs)
    mixture[0] = mixed.astype(mixture.dtype)
    totals[0] = logs


def attend_back_kernel(
    heads,
    scaling,
    queries,
    near_a,
    near_b,
    near_c,
    near_d,
    masks,
    totals,
    grad_mix,
    grad_q,
    grad_a,
    grad_b,
    grad_c,
    grad_d,
    sums,
):
    nears = (near_a, near_b, near_c, near_d)
    lane = lax.broadcasted_iota(jnp.int32, totals.shape[1:], 1)
    grad_query = jnp.zeros(grad_q.shape[1:], jnp.float32)
    for head in range(heads):
        mask = masks[head : head + 1]
        query = queries[0] * mask
        grad_out = grad_mix[0] * mask
        log_total = jnp.sum(jnp.where(lane == head, totals[0], 0.0), -1, keepdims=True)
        weights = [jnp.exp(dot_rows(query, near[0, 0]) * scaling - log_total) for near in nears]
        grad_w = [dot_rows(grad_out, near[1, 0]) for near in nears]
        inner = functools.reduce(
            jnp.add, [jnp.sum(w * g, -1, keepdims=True) for w, g in zip(weights, grad_w)]
        )
        for at, near in enumerate(nears):
            grad_scores = (weights[at] * (grad_w[at] - inner)).astype(jnp.bfloat16)
            grad_query += jnp.dot(grad_scores, near[0, 0] * mask, preferred_element_type=jnp.float32)
            grad_key = dot_cols(grad_scores, query)
            grad_value = dot_cols(weights[at].astype(jnp.bfloat16), grad_out)
            if head == 0:
                sums[at, 0] = grad_key
                sums[at, 1] = grad_value
            else:
                sums[at, 0] += grad_key
                sums[at, 1] += grad_value
    grad_q[0] = grad_query * scaling
    for at, out in enumerate((grad_a, grad_b, grad_c, grad_d)):
        out[0, 0] = (sums[at, 0] * scaling).astype(out.dtype)
        out[1, 0] = sums[at, 1].astype(out.dtype)


def text_kernel(head_dim, text, gains, same, keys_values):
    for group in range(2):
        hat, _ = head_hat(text[group, 0, 0], same[...], head_dim)
        keys_values[group, 0, 0] = (hat * gains[1:2]).astype(keys_values.dtype)
        keys_values[group, 1, 0] = text[group, 1, 0].astype(keys_values.dtype)


def text_back_kernel(head_dim, text, grads, gains, same, grad_text, gain_sums):
    width = grad_text.shape[4]
    gain_k = jnp.zeros((1, width), jnp.float32)
    for group in range(2):
        hat, scale = head_hat(text[group, 0, 0], same[...], head_dim)
        grad = grads[group, 0, 0]
        gain_k += jnp.sum(grad * hat, 0, keepdims=True)
        grad = head_hat_back(hat, scale, grad * gains[1:2], same[...], head_dim)
        grad_text[group, 0, 0] = grad.astype(grad_text.dtype)
        grad_text[group, 1, 0] = grads[group, 1, 0].astype(grad_text.dtype)
    accumulate(gain_sums, jnp.concatenate([gain_k, jnp.zeros((7, width), jnp.float32)], 0))


def cross_kernel(heads, head_dim, scaling, pre, text, present, gains, same, masks, mixture, totals):
    lane = lax.broadcasted_iota(jnp.int32, totals.shape[2:], 1)
    allowed = present[0] > 0
    for group in range(2):
        hat, _ = head_hat(pre[group, 0], same[...], head_dim)
        queries = (hat * gains[0:1]).astype(jnp.bfloat16)
        keys, values = text[group, 0, 0], text[group, 1, 0]
        mixed = jnp.zeros(mixture.shape[2:], jnp.float32)
        logs = jnp.zeros(totals.shape[2:], jnp.float32)
        for head in range(heads):
            mask = masks[head : head + 1]
            scores = jnp.where(allowed, dot_rows(queries * mask, keys) * scaling, -1e30)
            highest = jnp.max(scores, -1, keepdims=True)
            expo = jnp.exp(scores - highest)
            total = jnp.sum(expo, -1, keepdims=True)
            weights = (expo * (1.0 / total)).astype(jnp.bfloat16)
            mixed += jnp.dot(weights, values * mask, preferred_element_type=jnp.float32)
            logs = jnp.where(lane == head, highest + jnp.log(total), logs)
        mixture[group, 0] = mixed.astype(mixture.dtype)
        totals[group, 0] = logs


def cross_back_kernel(
    heads,
    head_dim,
    scaling,
    pre,
    text,
    present,
    gains,
    same,
    masks,
    totals,
    grad_mix,
    grad_pre,
    grad_text,
    gain_sums,
):
    lane = lax.broadcasted_iota(jnp.int32, totals.shape[2:], 1)
    allowed = present[0] > 0
    width = grad_pre.shape[3]
    gain_q = jnp.zeros((1, width), jnp.float32)
    for group in range(2):
        q_hat, q_scale = head_hat(pre[group, 0], same[...], head_dim)
        queries = (q_hat * gains[0:1]).astype(jnp.bfloat16)
        keys, values = text[group, 0, 0], text[group, 1, 0]
        grad_q = jnp.zeros(grad_pre.shape[2:], jnp.float32)
        for head in range(heads):
            mask = masks[head : head + 1]
            query = queries * mask
            grad_out = grad_mix[group, 0] * mask
            log_total = jnp.sum(jnp.where(lane == head, totals[group, 0], 0.0), -1, keepdims=True)
            scores = jnp.where(allowed, dot_rows(query, keys) * scaling, -1e30)
            weights = jnp.exp(scores - log_total)
            grad_w = dot_rows(grad_out, values)
            inner = jnp.sum(weights * grad_w, -1, keepdims=True)
            grad_scores = (weights * (grad_w - inner)).astype(jnp.bfloat16)
            grad_q += jnp.dot(grad_scores, keys * mask, preferred_element_type=jnp.float32)
            grad_k = dot_cols(grad_scores, query) * scaling
            grad_v = dot_cols(weights.astype(jnp.bfloat16), grad_out)
            if head == 0:
                grad_text[group, 0, 0] = grad_k
                grad_text[group, 1, 0] = grad_v
            else:
                grad_text[group, 0, 0] += grad_k
                grad_text[group, 1, 0] += grad_v
        grad_q = grad_q * scaling
        gain_q += jnp.sum(grad_q * q_hat, 0, keepdims=True)
        grad_q = head_hat_back(q_hat, q_scale, grad_q * gains[0:1], same[...], head_dim)
        grad_pre[group, 0] = grad_q.astype(grad_pre.dtype)
    accumulate(gain_sums, jnp.concatenate([gain_q, jnp.zeros((7, width), jnp.float32)], 0))


def whole(array):
    rank = len(array.shape)
    return pl.BlockSpec(array.shape, lambda pack: (0,) * rank)


def by_pack(array, axis, depth=1):
    shape = array.shape[:axis] + (depth,) + array.shape[axis + 1 :]
    rank = len(shape)
    return pl.BlockSpec(shape, lambda pack: tuple(pack if at == axis else 0 for at in range(rank)))


def per_pack(body, packs, inputs, outputs, flops, scratch=()):
    ins, in_specs, out_specs, shapes = [], [], [], []
    for array, axis, depth in inputs:
        ins.append(array)
        in_specs.append(whole(array) if axis is None else by_pack(array, axis, depth))
    for shape, dtype, axis, depth in outputs:
        spec = jax.ShapeDtypeStruct(shape, dtype)
        shapes.append(spec)
        out_specs.append(whole(spec) if axis is None else by_pack(spec, axis, depth))
    moved = sum(math.prod(a.shape) * a.dtype.itemsize for a in ins + shapes)
    return pl.pallas_call(
        body,
        grid=(packs,),
        in_specs=in_specs,
        out_specs=out_specs,
        out_shape=shapes,
        scratch_shapes=scratch,
        cost_estimate=pl.CostEstimate(flops=flops, bytes_accessed=moved, transcendentals=0),
        compiler_params=pltpu.CompilerParams(
            dimension_semantics=("arbitrary",), vmem_limit_bytes=48 * 1024 * 1024
        ),
    )(*ins)


def shards(
    latent,
    skip_in,
    context,
    image_ids,
    text_mask,
    patch_weight,
    skip_gain,
    skip_weight,
    norm_gains,
    qkv_weight,
    qk_gains,
    out_weight,
    cq_weight,
    ckv_weight,
    cout_weight,
    up_weight,
    down_weight,
    final_weight,
    cotangent,
):
    pack_count = latent.shape[0]
    in_channels = latent.shape[1]
    out_channels = cotangent.shape[1]
    tile_side = image_ids.shape[1]
    cells = tile_side * tile_side
    row_total = pack_count * cells
    model_width = skip_weight.shape[1]
    head_dim = qk_gains.shape[1]
    true_width = qkv_weight.shape[2]
    local_heads = true_width // head_dim
    head_width = -(-true_width // 128) * 128
    spare = head_width - true_width
    both_channels = in_channels + out_channels
    half_cells = cells // 2
    quarter_cells = cells // 4
    half_total = row_total // 2
    quarter_total = row_total // 4
    text_width = context.shape[2]
    tiles = math.prod(lax.axis_size(axis) for axis in TILES)
    upper, lower = lax.axis_index("zh"), lax.axis_index("zl")
    scaling = 1.0 / math.sqrt(head_dim)
    bf16 = jnp.bfloat16

    def my_half(values):
        shape = values.shape[1:]
        cut = pick(values.reshape(pack_count, 2, half_cells, *shape), upper, 1)
        return cut.reshape(half_total, *shape)

    def other_half(values):
        shape = values.shape[1:]
        cut = pick(values.reshape(pack_count, 2, half_cells, *shape), 1 - upper, 1)
        return cut.reshape(half_total, *shape)

    def both_halves(mine, other):
        shape = mine.shape[1:]
        mine = mine.reshape(pack_count, half_cells, *shape)
        other = other.reshape(pack_count, half_cells, *shape)
        first = jnp.where(upper == 0, mine, other)
        second = jnp.where(upper == 0, other, mine)
        return jnp.stack([first, second], 1).reshape(row_total, *shape)

    stacked = jnp.concatenate([latent, cotangent], 1)
    rows_axes, cols_axes = ("x", "core"), ("chi", "clo")
    lower_rim = from_behind(stacked[:, :, :1, :], rows_axes, -1)
    right_rim = from_behind(stacked[:, :, :, :1], cols_axes, -1)
    corner = from_corner(stacked[:, :, :1, :1])
    lower_rim = jnp.concatenate([lower_rim, corner], 3)[:, :, :, 1:]
    stacked = jnp.concatenate([stacked, right_rim], 3)[:, :, 1:, 1:]
    stacked = jnp.concatenate([stacked, lower_rim], 2)
    pieces = stacked.reshape(pack_count, both_channels, tile_side, 2, tile_side, 2)
    pieces = pieces.transpose(0, 2, 4, 1, 3, 5).reshape(row_total, both_channels * 4)
    patches = pieces[:, : in_channels * 4]
    grad_result = my_half(pieces[:, in_channels * 4 :])

    def spread_heads(values):
        return jnp.pad(jnp.tile(values, (1, local_heads)), ((0, 0), (0, spare)))

    qkv_wide = jnp.pad(qkv_weight, ((0, 0), (0, 0), (0, spare)))
    ckv_wide = jnp.pad(ckv_weight, ((0, 0), (0, 0), (0, spare)))
    out_tall, cout_tall, cq_tall = [
        jnp.pad(weight, ((0, spare), (0, 0))) for weight in (out_weight, cout_weight, cq_weight.T)
    ]
    token_index = jnp.arange(cells, dtype=jnp.int32)
    row_pos = lax.axis_index("core") * tile_side + token_index // tile_side
    col_pos = lax.axis_index("clo") * tile_side + token_index % tile_side
    cosine, sine = rope_tables(row_pos, col_pos, head_dim)
    cosine, sine = spread_heads(cosine), spread_heads(sine)
    lanes = jnp.arange(head_width, dtype=jnp.int32)
    head_of, place = lanes // head_dim, lanes % head_dim
    same = (head_of[:, None] == head_of[None, :]).astype(bf16)
    quarter = head_dim // 4
    ahead = (place // quarter % 2 == 0)[None, :]
    turn = jnp.where(
        ahead,
        -(lanes[:, None] == lanes[None, :] + quarter).astype(bf16),
        (lanes[:, None] == lanes[None, :] - quarter).astype(bf16),
    )
    masks = (jnp.arange(8, dtype=jnp.int32)[:, None] == head_of[None, :]).astype(bf16)
    flat_gains = spread_heads(jnp.pad(qk_gains, ((0, 4), (0, 0))))
    self_gains, cross_gains = flat_gains, jnp.roll(flat_gains, -2, 0)

    embed = project(patches, patch_weight)
    joined = jnp.concatenate(
        [embed, skip_in.reshape(row_total, model_width).astype(jnp.float32)], 1
    )
    normed = scaled_norm(joined, skip_gain).astype(bf16)
    slices = [sharer_slice(weight) for weight in (out_tall, cout_tall, cq_tall)]
    moved = swapped(jnp.stack(slices), "zh")
    gathered = lax.all_gather(after(moved, normed), SHARERS, axis=0, tiled=False)
    out_other, cout_other, cq_other = [
        gathered[:, at].reshape(head_width, model_width) for at in range(3)
    ]
    hidden = project(normed, skip_weight)
    ckv_other = partner_shard(ckv_wide.reshape(2 * text_width, head_width), hidden)
    out_pair = (out_tall, out_other)
    cq_pair = (cq_tall, cq_other)
    ckv_pair = (ckv_wide, ckv_other.reshape(ckv_wide.shape))
    cout_pair = (cout_tall, cout_other)
    n_one = scaled_norm(hidden, norm_gains[0]).astype(bf16)
    projected = jnp.einsum("rd,sde->sre", n_one, qkv_wide, preferred_element_type=jnp.float32)
    tile_flat = (pack_count, cells, head_width)
    near_flat = (2, pack_count, cells, head_width)
    queries, near_own = per_pack(
        functools.partial(turn_kernel, head_dim),
        pack_count,
        [
            (projected, 1, cells),
            (cosine, None, 1),
            (sine, None, 1),
            (self_gains, None, 1),
            (same, None, 1),
            (turn, None, 1),
        ],
        [(tile_flat, bf16, 0, 1), (near_flat, bf16, 1, 1)],
        row_total * head_width * head_width * 36,
    )
    up_both = jnp.concatenate([up_weight, partner_shard(up_weight, near_own)], 1)
    down_both = jnp.concatenate([down_weight, partner_shard(down_weight, near_own)], 0)
    nears = (near_own,) + tuple(to_partners(near_own) for to_partners in PARTNERS)
    near_args = [(near, 1, 1) for near in nears]
    self_flops = row_total * 4 * cells * head_width * local_heads * 4
    mixture, self_totals = per_pack(
        functools.partial(attend_kernel, local_heads, scaling),
        pack_count,
        [(queries, 0, 1), *near_args, (masks, None, 1)],
        [(tile_flat, bf16, 0, 1), ((pack_count, cells, 128), jnp.float32, 0, 1)],
        self_flops,
    )
    mixture = mixture.reshape(row_total, head_width)
    mix_pair = (my_half(mixture), swapped(other_half(mixture), "zh"))

    def joint(lefts, rights):
        return project(lefts[0], rights[0]) + project(lefts[1], rights[1])

    def joint_back(grads, weights):
        return back_dot(grads[0], weights[0]) + back_dot(grads[1], weights[1])

    x_one = my_half(hidden) + pair_sum(joint(mix_pair, out_pair))
    n_two = scaled_norm(x_one, norm_gains[1]).astype(bf16)
    caption = after(image_ids[:, 0, 0], near_own)
    text_len = context.shape[1]
    padding = -text_len % 128
    padded_len = text_len + padding
    chosen = jnp.pad(context[caption], ((0, 0), (0, padding), (0, 0)))
    present = jnp.pad((text_mask[caption] > 0).astype(jnp.float32), ((0, 0), (0, padding)))
    present = present[:, None, :]
    text_pre = jnp.stack(
        [
            jnp.einsum("ptc,sce->spte", chosen, weight, preferred_element_type=jnp.float32)
            for weight in ckv_pair
        ]
    )
    cross_pre = jnp.stack([back_dot(n_two, weight) for weight in cq_pair])
    cross_pre = cross_pre.reshape(2, pack_count, half_cells, head_width)
    (text_near,) = per_pack(
        functools.partial(text_kernel, head_dim),
        pack_count,
        [(text_pre, 2, 1), (cross_gains, None, 1), (same, None, 1)],
        [(text_pre.shape, bf16, 2, 1)],
        text_pre.size * head_width * 4,
    )
    cross_args = [
        (cross_pre, 1, 1),
        (text_near, 2, 1),
        (present, 0, 1),
        (cross_gains, None, 1),
        (same, None, 1),
        (masks, None, 1),
    ]
    cross_flat = (2, pack_count, half_cells, head_width)
    cross_flops = half_total * padded_len * head_width * local_heads * 8
    cross_mix, cross_totals = per_pack(
        functools.partial(cross_kernel, local_heads, head_dim, scaling),
        pack_count,
        cross_args,
        [(cross_flat, bf16, 1, 1), ((2, pack_count, half_cells, 128), jnp.float32, 1, 1)],
        cross_flops,
    )
    cross_mixes = [cross_mix[group].reshape(half_total, head_width) for group in range(2)]
    x_two = x_one + pair_sum(joint(cross_mixes, cout_pair))
    n_three = scaled_norm(x_two, norm_gains[2]).astype(bf16)
    up_pre = project(n_three, up_both)
    act = jax.nn.gelu(up_pre, approximate=True).astype(bf16)
    x_three = x_two + pair_sum(project(act, down_both))
    n_four = norm_rows(x_three).astype(bf16)
    result = project(n_four, final_weight).astype(bf16)
    result = both_halves(result, swapped(result, "zh"))
    grad_final = outer_sum(n_four, grad_result)
    unused, pull = jax.vjp(norm_rows, x_three)
    grad_stream = pull(back_dot(grad_result, final_weight))[0]
    branch = grad_stream.astype(bf16)
    unused, pull = jax.vjp(functools.partial(jax.nn.gelu, approximate=True), up_pre)
    grad_up_pre = pull(back_dot(branch, down_both))[0].astype(bf16)
    grad_down = outer_sum(branch, act).astype(bf16)
    grad_up = outer_sum(n_three, grad_up_pre).astype(bf16)
    grad_n_three = pair_sum(back_dot(grad_up_pre, up_both), (grad_down, grad_up))

    def scattered(grads):
        return lax.psum_scatter(grads, TILES, scatter_dimension=0, tiled=True)

    mlp_shares = (scattered(grad_down), scattered(grad_up))
    unused, pull = jax.vjp(scaled_norm, x_two, norm_gains[2])
    grad_input, gain_three = pull(grad_n_three)
    grad_stream = grad_stream + grad_input
    branch = grad_stream.astype(bf16)
    grad_cmix = jnp.stack([back_dot(branch, weight).astype(bf16) for weight in cout_pair])
    grad_cq, grad_text, cross_sums = per_pack(
        functools.partial(cross_back_kernel, local_heads, head_dim, scaling),
        pack_count,
        [*cross_args, (cross_totals, 1, 1), (grad_cmix.reshape(cross_flat), 1, 1)],
        [
            (cross_flat, bf16, 1, 1),
            (text_pre.shape, jnp.float32, 2, 1),
            ((8, head_width), jnp.float32, None, 1),
        ],
        3 * cross_flops,
    )
    grad_cqs = [grad_cq[group].reshape(half_total, head_width) for group in range(2)]
    grad_couts = [outer_sum(branch, mix).astype(bf16) for mix in cross_mixes]
    grad_cq_ws = [outer_sum(n_two, grad).astype(bf16) for grad in grad_cqs]
    grad_n_two = pair_sum(
        project(grad_cqs[0], cq_pair[0]) + project(grad_cqs[1], cq_pair[1]),
        (grad_couts, grad_cq_ws),
    )
    grad_text, text_sums = per_pack(
        functools.partial(text_back_kernel, head_dim),
        pack_count,
        [(text_pre, 2, 1), (grad_text, 2, 1), (cross_gains, None, 1), (same, None, 1)],
        [(text_pre.shape, bf16, 2, 1), ((8, head_width), jnp.float32, None, 1)],
        text_pre.size * head_width * 8,
    )
    grad_ckvs = [
        jnp.einsum(
            "ptc,pte->ce", chosen, grad_text[group, side], preferred_element_type=jnp.float32
        ).astype(bf16)
        for group in range(2)
        for side in range(2)
    ]
    narrow = grad_final.astype(bf16).reshape(tiles, -1, 4 * out_channels).transpose(0, 2, 1)
    narrow = jnp.pad(narrow, ((0, 0), (0, 0), (0, head_width - narrow.shape[2])))
    narrow = narrow.reshape(-1, head_width)
    mine = [grad_couts[0], grad_cq_ws[0], grad_ckvs[0], grad_ckvs[1]]
    other = [grad_couts[1], grad_cq_ws[1], grad_ckvs[2], grad_ckvs[3]]
    cross_steps = tile_sums(mine + [narrow] + other)
    cross_shares = cross_steps[2]
    unused, pull = jax.vjp(scaled_norm, x_one, norm_gains[1])
    grad_input, gain_two = pull(grad_n_two)
    grad_stream = grad_stream + grad_input
    branch = grad_stream.astype(bf16)
    grad_amixes = [back_dot(branch, weight).astype(bf16) for weight in out_pair]
    grad_amix = both_halves(grad_amixes[0], swapped(grad_amixes[1], "zh"))
    grad_outs = [outer_sum(branch, mix).astype(bf16) for mix in mix_pair]
    down_mine, down_other = jnp.split(mlp_shares[0], 2, 1)
    up_mine, up_other = jnp.split(mlp_shares[1], 2, 1)
    down_other, up_other = [swapped(after(x, grad_amix), "zh") for x in (down_other, up_other)]
    grad_q, *grad_nears = per_pack(
        functools.partial(attend_back_kernel, local_heads, scaling),
        pack_count,
        [
            (queries, 0, 1),
            *near_args,
            (masks, None, 1),
            (self_totals, 0, 1),
            (after(grad_amix.reshape(tile_flat), cross_steps[0]), 0, 1),
        ],
        [(tile_flat, jnp.float32, 0, 1), (near_flat, jnp.float32, 1, 1)]
        + [(near_flat, bf16, 1, 1)] * 3,
        self_flops * 5 // 2,
        [pltpu.VMEM((4, 2, cells, head_width), jnp.float32)],
    )
    arrived = [to_partners(grad) for to_partners, grad in zip(PARTNERS, grad_nears[1:])]
    arrived = after(arrived, (down_other, up_other, grad_outs, cross_steps[1]))
    grad_proj, self_sums = per_pack(
        functools.partial(turn_back_kernel, head_dim),
        pack_count,
        [
            (projected, 1, cells),
            (grad_q, 0, 1),
            (grad_nears[0], 1, 1),
            *[(grad, 1, 1) for grad in arrived],
            (cosine, None, 1),
            (sine, None, 1),
            (self_gains, None, 1),
            (same, None, 1),
            (turn.T, None, 1),
        ],
        [(projected.shape, bf16, 1, cells), ((8, head_width), jnp.float32, None, 1)],
        row_total * head_width * head_width * 60,
    )
    grad_n_one = jnp.einsum("sre,sde->rd", grad_proj, qkv_wide, preferred_element_type=jnp.float32)
    grad_qkvs = [outer_sum(n_one, grad_proj[part]).astype(bf16) for part in range(3)]
    self_steps = tile_sums(grad_outs + grad_qkvs)
    self_shares = self_steps[2]
    fine = grad_n_one.astype(bf16).reshape(pack_count, 2, 2, quarter_cells, model_width)
    kept = pick(fine, lower, 2).astype(jnp.float32)
    facing = after(swapped(pick(fine, 1 - lower, 2), "zl"), (grad_qkvs, cross_shares))
    kept = kept + facing.astype(jnp.float32)
    sent = swapped(pick(kept, 1 - upper, 1).astype(bf16), "zh")
    sent = after(sent, self_steps[0]).astype(jnp.float32)
    grad_n_one = (pick(kept, upper, 1) + sent).reshape(quarter_total, model_width)

    def my_quarter(half_rows):
        cut = pick(half_rows.reshape(pack_count, 2, quarter_cells, model_width), lower, 1)
        return cut.reshape(quarter_total, model_width)

    unused, pull = jax.vjp(scaled_norm, my_quarter(my_half(hidden)), norm_gains[0])
    grad_input, gain_one = pull(grad_n_one)
    branch = (my_quarter(grad_stream) + grad_input).astype(bf16)
    quarter = branch.reshape(pack_count, quarter_cells, model_width)

    def in_order(mine, other, index, axis):
        first = jnp.where(index == 0, mine, other)
        second = jnp.where(index == 0, other, mine)
        return jnp.stack([first, second], axis)

    branch = in_order(quarter, swapped(quarter, "zh"), upper, 1)
    facing = after(swapped(branch, "zl"), self_steps[1])
    branch = in_order(branch, facing, lower, 2).reshape(row_total, model_width)

    share_at = (2 * upper + lower) * true_width
    my_share = lax.dynamic_slice_in_dim(branch, share_at, true_width, 1)
    my_share = jnp.pad(my_share, ((0, 0), (0, spare)))
    grad_skip_w = outer_sum(normed, my_share).astype(bf16)
    skip_steps = tile_sums([grad_skip_w])
    skip_shares = skip_steps[2]
    branch = after(branch, grad_skip_w)
    unused, pull = jax.vjp(scaled_norm, joined, skip_gain)
    grad_joined, gain_skip = pull(back_dot(branch, skip_weight))
    grad_skip = grad_joined[:, model_width:].astype(bf16).reshape(skip_in.shape)
    grad_embed = grad_joined[:, :model_width].astype(bf16)
    grad_patch_w = outer_sum(grad_embed, patches)
    grad_patches = back_dot(grad_embed, patch_weight).astype(bf16)
    def with_partner(mine, other):
        other = after(swapped(after(other, branch), "zh"), gain_skip)
        return mine.astype(jnp.float32) + other.astype(jnp.float32)

    tile_rows = model_width // tiles
    sum_down = (down_mine.astype(jnp.float32) + down_other.astype(jnp.float32)).T
    sum_up = up_mine.astype(jnp.float32) + up_other.astype(jnp.float32)
    narrow_rows = 4 * out_channels
    near_rows = (cross_shares.shape[0] - narrow_rows) // 2
    far = [cross_shares[near_rows + narrow_rows :], cross_shares[near_rows:-near_rows]]
    cross_total = with_partner(cross_shares[:-near_rows], jnp.concatenate(far, 0))
    sum_cout = cross_total[:tile_rows, :true_width].T
    sum_cq = cross_total[tile_rows : 2 * tile_rows, :true_width]
    sum_final = cross_total[-4 * out_channels :, :tile_rows].T
    sum_ckv = cross_total[2 * tile_rows : -4 * out_channels, :true_width].reshape(
        2, -1, true_width
    )
    sum_out = with_partner(self_shares[:tile_rows], self_shares[tile_rows : 2 * tile_rows])
    sum_out = sum_out[:, :true_width].T
    sum_qkv = self_shares[2 * tile_rows :, :true_width].astype(jnp.float32)
    sum_qkv = sum_qkv.reshape(3, tile_rows, true_width)
    placed = jnp.concatenate([result, grad_patches], 1)
    placed = placed.reshape(pack_count, tile_side, tile_side, both_channels, 2, 2).transpose(
        0, 3, 1, 4, 2, 5
    )
    placed = placed.reshape(pack_count, both_channels, 2 * tile_side, 2 * tile_side)
    placed = jnp.pad(placed, ((0, 0), (0, 0), (1, 0), (1, 0)))
    moved_cols = from_behind(placed[:, :, :, -1:], ("chi", "clo"), 1)
    placed = jnp.concatenate([moved_cols, placed[:, :, :, 1:-1]], 3)
    moved_rows = from_behind(placed[:, :, -1:, :], ("x", "core"), 1)
    placed = jnp.concatenate([moved_rows, placed[:, :, 1:-1, :]], 2)
    out_latent = placed[:, :out_channels]
    grad_latent = placed[:, out_channels:]
    qk_parts = jnp.concatenate([self_sums[:2], cross_sums[:1], text_sums[:1]], 0)
    qk_parts = jnp.sum(qk_parts[:, :true_width].reshape(4, local_heads, head_dim), 1).reshape(-1)
    gains = [gain_one, 0.5 * gain_two, 0.5 * gain_three, 0.25 * gain_skip[:model_width]]
    gains = gains + [
        0.25 * gain_skip[model_width:],
        jnp.pad(qk_parts, (0, model_width - qk_parts.shape[0])),
    ]
    gains = everyones_sum(after(jnp.stack(gains), skip_steps[1]))
    gains_total = gains[:3]
    skip_gain_total = gains[3:5].reshape(-1)
    qk_total = gains[5, : 4 * head_dim].reshape(4, head_dim)
    sum_skip = lax.all_gather(skip_shares, ("zh", "zl"), axis=0, tiled=False)
    sum_skip = sum_skip[:, :, :true_width].transpose(1, 0, 2).reshape(-1, model_width)
    sum_patch = tile_sums([grad_patch_w.astype(bf16)])[2].astype(jnp.float32).T
    return (
        out_latent,
        grad_latent,
        grad_skip,
        sum_patch,
        skip_gain_total,
        sum_skip.astype(jnp.float32),
        gains_total,
        sum_qkv,
        qk_total,
        sum_out,
        sum_cq,
        sum_ckv,
        sum_cout,
        sum_up,
        sum_down,
        sum_final,
    )


def solution(mesh):
    rows, cols, heads = mesh.devices.shape
    fine = Mesh(
        mesh.devices.reshape(rows // 2, 2, cols // 2, 2, heads // 2, 2),
        ("x", "core", "chi", "clo", "zh", "zl"),
    )
    rows, cols, heads = ("x", "core"), ("chi", "clo"), ("zh", "zl")
    in_specs = (
        P(None, None, rows, cols),
        P(None, rows, cols, None),
        P(),
        P(None, rows, cols),
        P(),
        P(),
        P(),
        P(),
        P(),
        P(None, None, heads),
        P(),
        P(heads, None),
        P(None, heads),
        P(None, None, heads),
        P(heads, None),
        P(None, heads),
        P(heads, None),
        P(),
        P(None, None, rows, cols),
    )
    out_specs = (
        P(None, None, rows, cols),
        P(None, None, rows, cols),
        P(None, rows, cols, None),
        P(None, TILES),
        P(),
        P(TILES, None),
        P(),
        P(None, TILES, heads),
        P(),
        P(heads, TILES),
        P(TILES, heads),
        P(None, TILES, heads),
        P(heads, TILES),
        P(TILES, heads),
        P(heads, TILES),
        P(TILES, None),
    )
    return jax.shard_map(shards, mesh=fine, in_specs=in_specs, out_specs=out_specs, check_vma=False)
```

```python
import functools
import math

import jax
import jax.numpy as jnp
from jax import lax
from jax.experimental import pallas as pl
from jax.experimental.pallas import tpu as pltpu
from jax.sharding import Mesh, PartitionSpec as P

EPSILON = 1e-06


TILES = ("x", "core", "chi", "clo")
SHARERS = ("x", "core", "clo")
EVERYONE = ("x", "core", "chi", "clo", "zh", "zl")


def swapped(value, axis):
    return lax.ppermute(value, axis, [(i, i ^ 1) for i in range(lax.axis_size(axis))])


def from_behind(value, axis, by):
    devices = math.prod(lax.axis_size(name) for name in axis)
    pairs = [(i, i + by) for i in range(devices) if 0 <= i + by < devices]
    return lax.ppermute(value, axis, pairs)


def pick(values, index, axis):
    return lax.dynamic_index_in_dim(values, index, axis, keepdims=False)


def after(value, others):
    return lax.optimization_barrier((value, others))[0]


def sharer_slice(weight):
    sharers = math.prod(lax.axis_size(axis) for axis in SHARERS)
    depth = weight.shape[0] // sharers
    return lax.dynamic_slice_in_dim(weight, lax.axis_index(SHARERS) * depth, depth, 0)


def tile_sums(parts):
    axes = ("x", "core", "chi", "clo")
    sizes = [lax.axis_size(axis) for axis in axes]
    tiles = math.prod(sizes)
    blocks = [part.reshape(*sizes, part.shape[0] // tiles, part.shape[1]) for part in parts]

    def halved(blocks, axis, at):
        here = lax.axis_index(axis)
        sent = jnp.concatenate([pick(block, 1 - here, at) for block in blocks], -2)
        kept = jnp.concatenate([pick(block, here, at) for block in blocks], -2)
        total = kept.astype(jnp.float32) + swapped(sent, axis).astype(jnp.float32)
        return lax.reduce_precision(total, 8, 7).astype(jnp.bfloat16)

    by_core = halved(blocks, "core", 1)
    by_x = halved([by_core], "x", 0)
    by_cols = halved([by_x], "clo", 1)
    if sizes[2] == 1:
        return by_core, by_x, by_cols[0]
    return by_core, by_x, lax.psum_scatter(by_cols, "chi", scatter_dimension=0, tiled=False)


def axes_sum(values, axes):
    for axis in axes:
        values = values + swapped(values, axis)
    return values if lax.axis_size("chi") == 1 else lax.psum(values, "chi")


def from_corner(value):
    sizes = [lax.axis_size(axis) for axis in ("x", "core", "chi", "clo")]
    rows, cols = sizes[0] * sizes[1], sizes[2] * sizes[3]
    pairs = [
        ((i + 1) * cols + j + 1, i * cols + j) for i in range(rows - 1) for j in range(cols - 1)
    ]
    return lax.ppermute(value, ("x", "core", "chi", "clo"), pairs)


def partner_shard(weight, earlier):
    piece = swapped(sharer_slice(weight), "zh")
    return lax.all_gather(after(piece, earlier), SHARERS, axis=0, tiled=True)


def to_core(value):
    return swapped(value, "core")


def to_side(value):
    return swapped(value, "clo")


def to_corner(value):
    pairs = [(i, 3 - i) for i in range(4)]
    return lax.ppermute(value, ("core", "clo"), pairs)


PARTNERS = (to_core, to_side, to_corner)


def pair_sum(partial, meanwhile=()):
    mine = lax.optimization_barrier(partial.astype(jnp.bfloat16))
    other = after(swapped(mine, "zl"), meanwhile)
    return mine.astype(jnp.float32) + other.astype(jnp.float32)


def norm_rows(values):
    center = values - jnp.mean(values, -1, keepdims=True)
    spread = jnp.mean(center * center, -1, keepdims=True)
    return center * lax.rsqrt(spread + EPSILON)


def scaled_norm(values, gain):
    return norm_rows(values) * gain


def rope_tables(row_pos, col_pos, head_dim):
    quarter = head_dim // 4
    freqs = 10000.0 ** (-jnp.arange(quarter, dtype=jnp.float32) / quarter)
    row_angle = row_pos.astype(jnp.float32)[:, None] * freqs[None, :]
    col_angle = col_pos.astype(jnp.float32)[:, None] * freqs[None, :]
    cosine = jnp.concatenate(
        [jnp.cos(row_angle), jnp.cos(row_angle), jnp.cos(col_angle), jnp.cos(col_angle)], -1
    )
    sine = jnp.concatenate(
        [jnp.sin(row_angle), jnp.sin(row_angle), jnp.sin(col_angle), jnp.sin(col_angle)], -1
    )
    return (cosine, sine)


def project(left, right):
    return jnp.dot(left, right, preferred_element_type=jnp.float32)


def outer_sum(left, right):
    return jnp.einsum("rd,re->de", left, right, preferred_element_type=jnp.float32)


def back_dot(grads, weight):
    return jnp.einsum("re,de->rd", grads, weight, preferred_element_type=jnp.float32)


def float_dot(left, right, parts=2):
    total = jnp.zeros((left.shape[0], right.shape[1]), jnp.float32)
    for _ in range(parts):
        part = left.astype(jnp.bfloat16)
        total += jnp.dot(part, right, preferred_element_type=jnp.float32)
        left = left - part.astype(jnp.float32)
    return total


def dot_rows(left, right):
    return lax.dot_general(left, right, (((1,), (1,)), ((), ())), preferred_element_type=jnp.float32)


def dot_cols(left, right):
    return lax.dot_general(left, right, (((0,), (0,)), ((), ())), preferred_element_type=jnp.float32)


def head_hat(values, same, head_dim):
    center = values - float_dot(values, same, 3) * (1.0 / head_dim)
    spread = float_dot(center * center, same) * (1.0 / head_dim)
    scale = lax.rsqrt(spread + EPSILON)
    return center * scale, scale


def head_hat_back(hat, scale, grads, same, head_dim):
    mean = float_dot(grads, same) * (1.0 / head_dim)
    along = float_dot(grads * hat, same) * (1.0 / head_dim)
    return scale * (grads - mean - hat * along)


def accumulate(ref, value):
    @pl.when(pl.program_id(0) == 0)
    def _():
        ref[...] = jnp.zeros_like(ref)

    ref[...] += value


def turn_kernel(head_dim, proj, cosine, sine, gains, same, turn, queries, near):
    for part in range(2):
        hat, _ = head_hat(proj[part], same[...], head_dim)
        scaled = hat * gains[part : part + 1]
        turned = scaled * cosine[...] + float_dot(scaled, turn[...]) * sine[...]
        if part == 0:
            queries[0] = turned.astype(queries.dtype)
        else:
            near[0, 0] = turned.astype(near.dtype)
    near[1, 0] = proj[2].astype(near.dtype)


def turn_back_kernel(
    head_dim, proj, grad_q, own, one, two, three, cosine, sine, gains, same, back, grads, gain_sums
):
    sums = []
    for part in range(2):
        if part == 0:
            grad = grad_q[0]
        else:
            grad = own[0, 0] + one[0, 0].astype(jnp.float32)
            grad = grad + two[0, 0].astype(jnp.float32) + three[0, 0].astype(jnp.float32)
        hat, scale = head_hat(proj[part], same[...], head_dim)
        grad = grad * cosine[...] + float_dot(grad * sine[...], back[...])
        sums.append(jnp.sum(grad * hat, 0, keepdims=True))
        grad = head_hat_back(hat, scale, grad * gains[part : part + 1], same[...], head_dim)
        grads[part] = grad.astype(grads.dtype)
    grad = own[1, 0] + one[1, 0].astype(jnp.float32)
    grad = grad + two[1, 0].astype(jnp.float32) + three[1, 0].astype(jnp.float32)
    grads[2] = grad.astype(grads.dtype)
    accumulate(gain_sums, jnp.concatenate(sums + [jnp.zeros((6, sums[0].shape[1]), jnp.float32)], 0))


def attend_kernel(heads, scaling, queries, near_a, near_b, near_c, near_d, masks, mixture, totals):
    nears = (near_a, near_b, near_c, near_d)
    lane = lax.broadcasted_iota(jnp.int32, totals.shape[1:], 1)
    mixed = jnp.zeros(mixture.shape[1:], jnp.float32)
    logs = jnp.zeros(totals.shape[1:], jnp.float32)
    for head in range(heads):
        mask = masks[head : head + 1]
        query = queries[0] * mask
        scores = [dot_rows(query, near[0, 0]) * scaling for near in nears]
        highest = functools.reduce(jnp.maximum, [jnp.max(s, -1, keepdims=True) for s in scores])
        expo = [jnp.exp(s - highest) for s in scores]
        total = functools.reduce(jnp.add, [jnp.sum(e, -1, keepdims=True) for e in expo])
        inverse = 1.0 / total
        for e, near in zip(expo, nears):
            weights = (e * inverse).astype(jnp.bfloat16)
            mixed += jnp.dot(weights, near[1, 0] * mask, preferred_element_type=jnp.float32)
        logs = jnp.where(lane == head, highest + jnp.log(total), logs)
    mixture[0] = mixed.astype(mixture.dtype)
    totals[0] = logs


def attend_back_kernel(
    heads,
    scaling,
    queries,
    near_a,
    near_b,
    near_c,
    near_d,
    masks,
    totals,
    grad_mix,
    grad_q,
    grad_a,
    grad_b,
    grad_c,
    grad_d,
    sums,
):
    nears = (near_a, near_b, near_c, near_d)
    lane = lax.broadcasted_iota(jnp.int32, totals.shape[1:], 1)
    grad_query = jnp.zeros(grad_q.shape[1:], jnp.float32)
    for head in range(heads):
        mask = masks[head : head + 1]
        query = queries[0] * mask
        grad_out = grad_mix[0] * mask
        log_total = jnp.sum(jnp.where(lane == head, totals[0], 0.0), -1, keepdims=True)
        weights = [jnp.exp(dot_rows(query, near[0, 0]) * scaling - log_total) for near in nears]
        grad_w = [dot_rows(grad_out, near[1, 0]) for near in nears]
        inner = functools.reduce(
            jnp.add, [jnp.sum(w * g, -1, keepdims=True) for w, g in zip(weights, grad_w)]
        )
        for at, near in enumerate(nears):
            grad_scores = (weights[at] * (grad_w[at] - inner)).astype(jnp.bfloat16)
            grad_query += jnp.dot(grad_scores, near[0, 0] * mask, preferred_element_type=jnp.float32)
            grad_key = dot_cols(grad_scores, query)
            grad_value = dot_cols(weights[at].astype(jnp.bfloat16), grad_out)
            if head == 0:
                sums[at, 0] = grad_key
                sums[at, 1] = grad_value
            else:
                sums[at, 0] += grad_key
                sums[at, 1] += grad_value
    grad_q[0] = grad_query * scaling
    for at, out in enumerate((grad_a, grad_b, grad_c, grad_d)):
        out[0, 0] = (sums[at, 0] * scaling).astype(out.dtype)
        out[1, 0] = sums[at, 1].astype(out.dtype)


def text_kernel(head_dim, text, gains, same, keys_values):
    for group in range(2):
        hat, _ = head_hat(text[group, 0, 0], same[...], head_dim)
        keys_values[group, 0, 0] = (hat * gains[1:2]).astype(keys_values.dtype)
        keys_values[group, 1, 0] = text[group, 1, 0].astype(keys_values.dtype)


def text_back_kernel(head_dim, text, grads, gains, same, grad_text, gain_sums):
    width = grad_text.shape[4]
    gain_k = jnp.zeros((1, width), jnp.float32)
    for group in range(2):
        hat, scale = head_hat(text[group, 0, 0], same[...], head_dim)
        grad = grads[group, 0, 0]
        gain_k += jnp.sum(grad * hat, 0, keepdims=True)
        grad = head_hat_back(hat, scale, grad * gains[1:2], same[...], head_dim)
        grad_text[group, 0, 0] = grad.astype(grad_text.dtype)
        grad_text[group, 1, 0] = grads[group, 1, 0].astype(grad_text.dtype)
    accumulate(gain_sums, jnp.concatenate([gain_k, jnp.zeros((7, width), jnp.float32)], 0))


def cross_kernel(heads, head_dim, scaling, pre, text, present, gains, same, masks, mixture, totals):
    lane = lax.broadcasted_iota(jnp.int32, totals.shape[2:], 1)
    allowed = present[0] > 0
    for group in range(2):
        hat, _ = head_hat(pre[group, 0], same[...], head_dim)
        queries = (hat * gains[0:1]).astype(jnp.bfloat16)
        keys, values = text[group, 0, 0], text[group, 1, 0]
        mixed = jnp.zeros(mixture.shape[2:], jnp.float32)
        logs = jnp.zeros(totals.shape[2:], jnp.float32)
        for head in range(heads):
            mask = masks[head : head + 1]
            scores = jnp.where(allowed, dot_rows(queries * mask, keys) * scaling, -1e30)
            highest = jnp.max(scores, -1, keepdims=True)
            expo = jnp.exp(scores - highest)
            total = jnp.sum(expo, -1, keepdims=True)
            weights = (expo * (1.0 / total)).astype(jnp.bfloat16)
            mixed += jnp.dot(weights, values * mask, preferred_element_type=jnp.float32)
            logs = jnp.where(lane == head, highest + jnp.log(total), logs)
        mixture[group, 0] = mixed.astype(mixture.dtype)
        totals[group, 0] = logs


def cross_back_kernel(
    heads,
    head_dim,
    scaling,
    pre,
    text,
    present,
    gains,
    same,
    masks,
    totals,
    grad_mix,
    grad_pre,
    grad_text,
    gain_sums,
):
    lane = lax.broadcasted_iota(jnp.int32, totals.shape[2:], 1)
    allowed = present[0] > 0
    width = grad_pre.shape[3]
    gain_q = jnp.zeros((1, width), jnp.float32)
    for group in range(2):
        q_hat, q_scale = head_hat(pre[group, 0], same[...], head_dim)
        queries = (q_hat * gains[0:1]).astype(jnp.bfloat16)
        keys, values = text[group, 0, 0], text[group, 1, 0]
        grad_q = jnp.zeros(grad_pre.shape[2:], jnp.float32)
        for head in range(heads):
            mask = masks[head : head + 1]
            query = queries * mask
            grad_out = grad_mix[group, 0] * mask
            log_total = jnp.sum(jnp.where(lane == head, totals[group, 0], 0.0), -1, keepdims=True)
            scores = jnp.where(allowed, dot_rows(query, keys) * scaling, -1e30)
            weights = jnp.exp(scores - log_total)
            grad_w = dot_rows(grad_out, values)
            inner = jnp.sum(weights * grad_w, -1, keepdims=True)
            grad_scores = (weights * (grad_w - inner)).astype(jnp.bfloat16)
            grad_q += jnp.dot(grad_scores, keys * mask, preferred_element_type=jnp.float32)
            grad_k = dot_cols(grad_scores, query) * scaling
            grad_v = dot_cols(weights.astype(jnp.bfloat16), grad_out)
            if head == 0:
                grad_text[group, 0, 0] = grad_k
                grad_text[group, 1, 0] = grad_v
            else:
                grad_text[group, 0, 0] += grad_k
                grad_text[group, 1, 0] += grad_v
        grad_q = grad_q * scaling
        gain_q += jnp.sum(grad_q * q_hat, 0, keepdims=True)
        grad_q = head_hat_back(q_hat, q_scale, grad_q * gains[0:1], same[...], head_dim)
        grad_pre[group, 0] = grad_q.astype(grad_pre.dtype)
    accumulate(gain_sums, jnp.concatenate([gain_q, jnp.zeros((7, width), jnp.float32)], 0))


def whole(array):
    rank = len(array.shape)
    return pl.BlockSpec(array.shape, lambda pack: (0,) * rank)


def by_pack(array, axis, depth=1):
    shape = array.shape[:axis] + (depth,) + array.shape[axis + 1 :]
    rank = len(shape)
    return pl.BlockSpec(shape, lambda pack: tuple(pack if at == axis else 0 for at in range(rank)))


def per_pack(body, packs, inputs, outputs, flops, scratch=()):
    ins, in_specs, out_specs, shapes = [], [], [], []
    for array, axis, depth in inputs:
        ins.append(array)
        in_specs.append(whole(array) if axis is None else by_pack(array, axis, depth))
    for shape, dtype, axis, depth in outputs:
        spec = jax.ShapeDtypeStruct(shape, dtype)
        shapes.append(spec)
        out_specs.append(whole(spec) if axis is None else by_pack(spec, axis, depth))
    moved = sum(math.prod(a.shape) * a.dtype.itemsize for a in ins + shapes)
    return pl.pallas_call(
        body,
        grid=(packs,),
        in_specs=in_specs,
        out_specs=out_specs,
        out_shape=shapes,
        scratch_shapes=scratch,
        cost_estimate=pl.CostEstimate(flops=flops, bytes_accessed=moved, transcendentals=0),
        compiler_params=pltpu.CompilerParams(
            dimension_semantics=("arbitrary",), vmem_limit_bytes=48 * 1024 * 1024
        ),
    )(*ins)


def shards(
    latent,
    skip_in,
    context,
    image_ids,
    text_mask,
    patch_weight,
    skip_gain,
    skip_weight,
    norm_gains,
    qkv_weight,
    qk_gains,
    out_weight,
    cq_weight,
    ckv_weight,
    cout_weight,
    up_weight,
    down_weight,
    final_weight,
    cotangent,
):
    pack_count = latent.shape[0]
    in_channels = latent.shape[1]
    out_channels = cotangent.shape[1]
    tile_side = image_ids.shape[1]
    cells = tile_side * tile_side
    row_total = pack_count * cells
    model_width = skip_weight.shape[1]
    head_dim = qk_gains.shape[1]
    true_width = qkv_weight.shape[2]
    local_heads = true_width // head_dim
    head_width = -(-true_width // 128) * 128
    spare = head_width - true_width
    both_channels = in_channels + out_channels
    half_cells = cells // 2
    quarter_cells = cells // 4
    half_total = row_total // 2
    quarter_total = row_total // 4
    text_width = context.shape[2]
    tiles = math.prod(lax.axis_size(axis) for axis in TILES)
    upper, lower = lax.axis_index("zh"), lax.axis_index("zl")
    scaling = 1.0 / math.sqrt(head_dim)
    bf16 = jnp.bfloat16

    def my_half(values):
        shape = values.shape[1:]
        cut = pick(values.reshape(pack_count, 2, half_cells, *shape), upper, 1)
        return cut.reshape(half_total, *shape)

    def other_half(values):
        shape = values.shape[1:]
        cut = pick(values.reshape(pack_count, 2, half_cells, *shape), 1 - upper, 1)
        return cut.reshape(half_total, *shape)

    def both_halves(mine, other):
        shape = mine.shape[1:]
        mine = mine.reshape(pack_count, half_cells, *shape)
        other = other.reshape(pack_count, half_cells, *shape)
        first = jnp.where(upper == 0, mine, other)
        second = jnp.where(upper == 0, other, mine)
        return jnp.stack([first, second], 1).reshape(row_total, *shape)

    stacked = jnp.concatenate([latent, cotangent], 1)
    rows_axes, cols_axes = ("x", "core"), ("chi", "clo")
    lower_rim = from_behind(stacked[:, :, :1, :], rows_axes, -1)
    right_rim = from_behind(stacked[:, :, :, :1], cols_axes, -1)
    corner = from_corner(stacked[:, :, :1, :1])
    lower_rim = jnp.concatenate([lower_rim, corner], 3)[:, :, :, 1:]
    stacked = jnp.concatenate([stacked, right_rim], 3)[:, :, 1:, 1:]
    stacked = jnp.concatenate([stacked, lower_rim], 2)
    pieces = stacked.reshape(pack_count, both_channels, tile_side, 2, tile_side, 2)
    pieces = pieces.transpose(0, 2, 4, 1, 3, 5).reshape(row_total, both_channels * 4)
    patches = pieces[:, : in_channels * 4]
    grad_result = my_half(pieces[:, in_channels * 4 :])

    def spread_heads(values):
        return jnp.pad(jnp.tile(values, (1, local_heads)), ((0, 0), (0, spare)))

    qkv_wide = jnp.pad(qkv_weight, ((0, 0), (0, 0), (0, spare)))
    ckv_wide = jnp.pad(ckv_weight, ((0, 0), (0, 0), (0, spare)))
    out_tall, cout_tall, cq_tall = [
        jnp.pad(weight, ((0, spare), (0, 0))) for weight in (out_weight, cout_weight, cq_weight.T)
    ]
    token_index = jnp.arange(cells, dtype=jnp.int32)
    row_pos = lax.axis_index("core") * tile_side + token_index // tile_side
    col_pos = lax.axis_index("clo") * tile_side + token_index % tile_side
    cosine, sine = rope_tables(row_pos, col_pos, head_dim)
    cosine, sine = spread_heads(cosine), spread_heads(sine)
    lanes = jnp.arange(head_width, dtype=jnp.int32)
    head_of, place = lanes // head_dim, lanes % head_dim
    same = (head_of[:, None] == head_of[None, :]).astype(bf16)
    quarter = head_dim // 4
    ahead = (place // quarter % 2 == 0)[None, :]
    turn = jnp.where(
        ahead,
        -(lanes[:, None] == lanes[None, :] + quarter).astype(bf16),
        (lanes[:, None] == lanes[None, :] - quarter).astype(bf16),
    )
    masks = (jnp.arange(8, dtype=jnp.int32)[:, None] == head_of[None, :]).astype(bf16)
    flat_gains = spread_heads(jnp.pad(qk_gains, ((0, 4), (0, 0))))
    self_gains, cross_gains = flat_gains, jnp.roll(flat_gains, -2, 0)

    embed = project(patches, patch_weight)
    joined = jnp.concatenate(
        [embed, skip_in.reshape(row_total, model_width).astype(jnp.float32)], 1
    )
    normed = scaled_norm(joined, skip_gain).astype(bf16)
    slices = [sharer_slice(weight) for weight in (out_tall, cout_tall, cq_tall)]
    moved = swapped(jnp.stack(slices), "zh")
    gathered = lax.all_gather(after(moved, normed), SHARERS, axis=0, tiled=False)
    out_other, cout_other, cq_other = [
        gathered[:, at].reshape(head_width, model_width) for at in range(3)
    ]
    hidden = project(normed, skip_weight)
    ckv_other = partner_shard(ckv_wide.reshape(2 * text_width, head_width), hidden)
    out_pair = (out_tall, out_other)
    cq_pair = (cq_tall, cq_other)
    ckv_pair = (ckv_wide, ckv_other.reshape(ckv_wide.shape))
    cout_pair = (cout_tall, cout_other)
    n_one = scaled_norm(hidden, norm_gains[0]).astype(bf16)
    projected = jnp.einsum("rd,sde->sre", n_one, qkv_wide, preferred_element_type=jnp.float32)
    tile_flat = (pack_count, cells, head_width)
    near_flat = (2, pack_count, cells, head_width)
    queries, near_own = per_pack(
        functools.partial(turn_kernel, head_dim),
        pack_count,
        [
            (projected, 1, cells),
            (cosine, None, 1),
            (sine, None, 1),
            (self_gains, None, 1),
            (same, None, 1),
            (turn, None, 1),
        ],
        [(tile_flat, bf16, 0, 1), (near_flat, bf16, 1, 1)],
        row_total * head_width * head_width * 36,
    )
    nears = (near_own,) + tuple(to_partners(near_own) for to_partners in PARTNERS)
    up_both = jnp.concatenate([after(up_weight, nears[1]), partner_shard(up_weight, near_own)], 1)
    down_both = jnp.concatenate([after(down_weight, nears[1]), partner_shard(down_weight, near_own)], 0)
    near_args = [(near, 1, 1) for near in nears]
    self_flops = row_total * 4 * cells * head_width * local_heads * 4
    mixture, self_totals = per_pack(
        functools.partial(attend_kernel, local_heads, scaling),
        pack_count,
        [(queries, 0, 1), *near_args, (masks, None, 1)],
        [(tile_flat, bf16, 0, 1), ((pack_count, cells, 128), jnp.float32, 0, 1)],
        self_flops,
    )
    mixture = mixture.reshape(row_total, head_width)
    mix_pair = (my_half(mixture), swapped(other_half(mixture), "zh"))

    def joint(lefts, rights):
        return project(lefts[0], rights[0]) + project(lefts[1], rights[1])

    def joint_back(grads, weights):
        return back_dot(grads[0], weights[0]) + back_dot(grads[1], weights[1])

    x_one = my_half(hidden) + pair_sum(joint(mix_pair, out_pair))
    n_two = scaled_norm(x_one, norm_gains[1]).astype(bf16)
    caption = after(image_ids[:, 0, 0], near_own)
    text_len = context.shape[1]
    padding = -text_len % 128
    padded_len = text_len + padding
    chosen = jnp.pad(context[caption], ((0, 0), (0, padding), (0, 0)))
    present = jnp.pad((text_mask[caption] > 0).astype(jnp.float32), ((0, 0), (0, padding)))
    present = present[:, None, :]
    text_pre = jnp.stack(
        [
            jnp.einsum("ptc,sce->spte", chosen, weight, preferred_element_type=jnp.float32)
            for weight in ckv_pair
        ]
    )
    cross_pre = jnp.stack([back_dot(n_two, weight) for weight in cq_pair])
    cross_pre = cross_pre.reshape(2, pack_count, half_cells, head_width)
    (text_near,) = per_pack(
        functools.partial(text_kernel, head_dim),
        pack_count,
        [(text_pre, 2, 1), (cross_gains, None, 1), (same, None, 1)],
        [(text_pre.shape, bf16, 2, 1)],
        text_pre.size * head_width * 4,
    )
    cross_args = [
        (cross_pre, 1, 1),
        (text_near, 2, 1),
        (present, 0, 1),
        (cross_gains, None, 1),
        (same, None, 1),
        (masks, None, 1),
    ]
    cross_flat = (2, pack_count, half_cells, head_width)
    cross_flops = half_total * padded_len * head_width * local_heads * 8
    cross_mix, cross_totals = per_pack(
        functools.partial(cross_kernel, local_heads, head_dim, scaling),
        pack_count,
        cross_args,
        [(cross_flat, bf16, 1, 1), ((2, pack_count, half_cells, 128), jnp.float32, 1, 1)],
        cross_flops,
    )
    cross_mixes = [cross_mix[group].reshape(half_total, head_width) for group in range(2)]
    x_two = x_one + pair_sum(joint(cross_mixes, cout_pair))
    n_three = scaled_norm(x_two, norm_gains[2]).astype(bf16)
    up_pre = project(n_three, up_both)
    act = jax.nn.gelu(up_pre, approximate=True).astype(bf16)
    x_three = x_two + pair_sum(project(act, down_both))
    n_four = norm_rows(x_three).astype(bf16)
    result = project(n_four, final_weight).astype(bf16)
    result = both_halves(result, swapped(result, "zh"))
    grad_final = outer_sum(n_four, grad_result)
    unused, pull = jax.vjp(norm_rows, x_three)
    grad_stream = pull(back_dot(grad_result, final_weight))[0]
    branch = grad_stream.astype(bf16)
    unused, pull = jax.vjp(functools.partial(jax.nn.gelu, approximate=True), up_pre)
    grad_up_pre = pull(back_dot(branch, down_both))[0].astype(bf16)
    grad_down = outer_sum(branch, act).astype(bf16)
    grad_up = outer_sum(n_three, grad_up_pre).astype(bf16)
    grad_n_three = pair_sum(back_dot(grad_up_pre, up_both), (grad_down, grad_up))

    def scattered(grads):
        return lax.psum_scatter(grads, TILES, scatter_dimension=0, tiled=True)

    mlp_shares = (scattered(grad_down), scattered(grad_up))
    unused, pull = jax.vjp(scaled_norm, x_two, norm_gains[2])
    grad_input, gain_three = pull(grad_n_three)
    grad_stream = grad_stream + grad_input
    branch = grad_stream.astype(bf16)
    grad_cmix = jnp.stack([back_dot(branch, weight).astype(bf16) for weight in cout_pair])
    grad_cq, grad_text, cross_sums = per_pack(
        functools.partial(cross_back_kernel, local_heads, head_dim, scaling),
        pack_count,
        [*cross_args, (cross_totals, 1, 1), (grad_cmix.reshape(cross_flat), 1, 1)],
        [
            (cross_flat, bf16, 1, 1),
            (text_pre.shape, jnp.float32, 2, 1),
            ((8, head_width), jnp.float32, None, 1),
        ],
        3 * cross_flops,
    )
    grad_cqs = [grad_cq[group].reshape(half_total, head_width) for group in range(2)]
    grad_couts = [outer_sum(branch, mix).astype(bf16) for mix in cross_mixes]
    grad_cq_ws = [outer_sum(n_two, grad).astype(bf16) for grad in grad_cqs]
    grad_n_two = pair_sum(
        project(grad_cqs[0], cq_pair[0]) + project(grad_cqs[1], cq_pair[1]),
        (grad_couts, grad_cq_ws),
    )
    grad_text, text_sums = per_pack(
        functools.partial(text_back_kernel, head_dim),
        pack_count,
        [(text_pre, 2, 1), (grad_text, 2, 1), (cross_gains, None, 1), (same, None, 1)],
        [(text_pre.shape, bf16, 2, 1), ((8, head_width), jnp.float32, None, 1)],
        text_pre.size * head_width * 8,
    )
    grad_ckvs = [
        jnp.einsum(
            "ptc,pte->ce", chosen, grad_text[group, side], preferred_element_type=jnp.float32
        ).astype(bf16)
        for group in range(2)
        for side in range(2)
    ]
    narrow = grad_final.astype(bf16).reshape(tiles, -1, 4 * out_channels).transpose(0, 2, 1)
    narrow = jnp.pad(narrow, ((0, 0), (0, 0), (0, head_width - narrow.shape[2])))
    narrow = narrow.reshape(-1, head_width)
    mine = [grad_couts[0], grad_cq_ws[0], grad_ckvs[0], grad_ckvs[1]]
    other = [grad_couts[1], grad_cq_ws[1], grad_ckvs[2], grad_ckvs[3]]
    cross_steps = tile_sums(mine + [narrow] + other)
    cross_shares = cross_steps[2]
    unused, pull = jax.vjp(scaled_norm, x_one, norm_gains[1])
    grad_input, gain_two = pull(grad_n_two)
    grad_stream = grad_stream + grad_input
    branch = grad_stream.astype(bf16)
    grad_amixes = [back_dot(branch, weight).astype(bf16) for weight in out_pair]
    grad_amix = both_halves(grad_amixes[0], swapped(grad_amixes[1], "zh"))
    grad_outs = [outer_sum(branch, mix).astype(bf16) for mix in mix_pair]
    down_mine, down_other = jnp.split(mlp_shares[0], 2, 1)
    up_mine, up_other = jnp.split(mlp_shares[1], 2, 1)
    down_other, up_other = [swapped(after(x, grad_amix), "zh") for x in (down_other, up_other)]
    grad_q, *grad_nears = per_pack(
        functools.partial(attend_back_kernel, local_heads, scaling),
        pack_count,
        [
            (queries, 0, 1),
            *near_args,
            (masks, None, 1),
            (self_totals, 0, 1),
            (after(grad_amix.reshape(tile_flat), cross_steps[0]), 0, 1),
        ],
        [(tile_flat, jnp.float32, 0, 1), (near_flat, jnp.float32, 1, 1)]
        + [(near_flat, bf16, 1, 1)] * 3,
        self_flops * 5 // 2,
        [pltpu.VMEM((4, 2, cells, head_width), jnp.float32)],
    )
    arrived = [to_partners(grad) for to_partners, grad in zip(PARTNERS, grad_nears[1:])]
    arrived = after(arrived, (down_other, up_other, grad_outs, cross_steps[1]))
    grad_proj, self_sums = per_pack(
        functools.partial(turn_back_kernel, head_dim),
        pack_count,
        [
            (projected, 1, cells),
            (grad_q, 0, 1),
            (grad_nears[0], 1, 1),
            *[(grad, 1, 1) for grad in arrived],
            (cosine, None, 1),
            (sine, None, 1),
            (self_gains, None, 1),
            (same, None, 1),
            (turn.T, None, 1),
        ],
        [(projected.shape, bf16, 1, cells), ((8, head_width), jnp.float32, None, 1)],
        row_total * head_width * head_width * 60,
    )
    grad_n_one = jnp.einsum("sre,sde->rd", grad_proj, qkv_wide, preferred_element_type=jnp.float32)
    grad_qkvs = [outer_sum(n_one, grad_proj[part]).astype(bf16) for part in range(3)]
    self_steps = tile_sums(grad_outs + grad_qkvs)
    self_shares = self_steps[2]
    fine = grad_n_one.astype(bf16).reshape(pack_count, 2, 2, quarter_cells, model_width)
    kept = pick(fine, lower, 2).astype(jnp.float32)
    facing = after(swapped(pick(fine, 1 - lower, 2), "zl"), (grad_qkvs, cross_shares))
    kept = kept + facing.astype(jnp.float32)
    sent = swapped(pick(kept, 1 - upper, 1).astype(bf16), "zh")
    sent = after(sent, self_steps[0]).astype(jnp.float32)
    grad_n_one = (pick(kept, upper, 1) + sent).reshape(quarter_total, model_width)

    def my_quarter(half_rows):
        cut = pick(half_rows.reshape(pack_count, 2, quarter_cells, model_width), lower, 1)
        return cut.reshape(quarter_total, model_width)

    unused, pull = jax.vjp(scaled_norm, my_quarter(my_half(hidden)), norm_gains[0])
    grad_input, gain_one = pull(grad_n_one)
    branch = (my_quarter(grad_stream) + grad_input).astype(bf16)
    quarter = branch.reshape(pack_count, quarter_cells, model_width)

    def in_order(mine, other, index, axis):
        first = jnp.where(index == 0, mine, other)
        second = jnp.where(index == 0, other, mine)
        return jnp.stack([first, second], axis)

    branch = in_order(quarter, swapped(quarter, "zh"), upper, 1)
    facing = after(swapped(branch, "zl"), self_steps[1])
    branch = in_order(branch, facing, lower, 2).reshape(row_total, model_width)

    share_at = (2 * upper + lower) * true_width
    my_share = lax.dynamic_slice_in_dim(branch, share_at, true_width, 1)
    my_share = jnp.pad(my_share, ((0, 0), (0, spare)))
    grad_skip_w = outer_sum(normed, my_share).astype(bf16)
    skip_steps = tile_sums([grad_skip_w])
    skip_shares = skip_steps[2]
    branch = after(branch, grad_skip_w)
    unused, pull = jax.vjp(scaled_norm, joined, skip_gain)
    grad_joined, gain_skip = pull(after(back_dot(branch, skip_weight), skip_steps[0]))
    grad_skip = grad_joined[:, model_width:].astype(bf16).reshape(skip_in.shape)
    grad_embed = grad_joined[:, :model_width].astype(bf16)
    grad_patch_w = outer_sum(grad_embed, patches)
    grad_patches = back_dot(grad_embed, patch_weight).astype(bf16)
    def with_partner(mine, other):
        other = after(swapped(after(other, branch), "zh"), gain_skip)
        return mine.astype(jnp.float32) + other.astype(jnp.float32)

    tile_rows = model_width // tiles
    sum_down = (down_mine.astype(jnp.float32) + down_other.astype(jnp.float32)).T
    sum_up = up_mine.astype(jnp.float32) + up_other.astype(jnp.float32)
    narrow_rows = 4 * out_channels
    near_rows = (cross_shares.shape[0] - narrow_rows) // 2
    far = [cross_shares[near_rows + narrow_rows :], cross_shares[near_rows:-near_rows]]
    cross_total = with_partner(cross_shares[:-near_rows], jnp.concatenate(far, 0))
    sum_cout = cross_total[:tile_rows, :true_width].T
    sum_cq = cross_total[tile_rows : 2 * tile_rows, :true_width]
    sum_final = cross_total[-4 * out_channels :, :tile_rows].T
    sum_ckv = cross_total[2 * tile_rows : -4 * out_channels, :true_width].reshape(
        2, -1, true_width
    )
    sum_out = with_partner(self_shares[:tile_rows], self_shares[tile_rows : 2 * tile_rows])
    sum_out = sum_out[:, :true_width].T
    sum_qkv = self_shares[2 * tile_rows :, :true_width].astype(jnp.float32)
    sum_qkv = sum_qkv.reshape(3, tile_rows, true_width)
    placed = jnp.concatenate([result, grad_patches], 1)
    placed = placed.reshape(pack_count, tile_side, tile_side, both_channels, 2, 2).transpose(
        0, 3, 1, 4, 2, 5
    )
    placed = placed.reshape(pack_count, both_channels, 2 * tile_side, 2 * tile_side)
    placed = jnp.pad(placed, ((0, 0), (0, 0), (1, 0), (1, 0)))
    moved_cols = from_behind(placed[:, :, :, -1:], ("chi", "clo"), 1)
    placed = jnp.concatenate([moved_cols, placed[:, :, :, 1:-1]], 3)
    moved_rows = from_behind(placed[:, :, -1:, :], ("x", "core"), 1)
    placed = jnp.concatenate([moved_rows, placed[:, :, 1:-1, :]], 2)
    out_latent = placed[:, :out_channels]
    grad_latent = placed[:, out_channels:]
    qk_parts = jnp.concatenate([self_sums[:2], cross_sums[:1], text_sums[:1]], 0)
    qk_parts = jnp.sum(qk_parts[:, :true_width].reshape(4, local_heads, head_dim), 1).reshape(-1)
    gains = [gain_one, 0.5 * gain_two, 0.5 * gain_three]
    gains = gains + [jnp.pad(qk_parts, (0, model_width - qk_parts.shape[0]))]
    gains = axes_sum(jnp.stack(gains), ("zl", "zh", "core", "x", "clo"))
    gains_total = gains[:3]
    qk_total = gains[3, : 4 * head_dim].reshape(4, head_dim)
    skip_gain_total = axes_sum(after(gain_skip.reshape(2, -1), skip_steps[1]), ("core", "x", "clo"))
    skip_gain_total = skip_gain_total.reshape(-1)
    sum_skip = lax.all_gather(skip_shares, ("zh", "zl"), axis=0, tiled=False)
    sum_skip = sum_skip[:, :, :true_width].transpose(1, 0, 2).reshape(-1, model_width)
    sum_patch = tile_sums([grad_patch_w.astype(bf16)])[2].astype(jnp.float32).T
    return (
        out_latent,
        grad_latent,
        grad_skip,
        sum_patch,
        skip_gain_total,
        sum_skip.astype(jnp.float32),
        gains_total,
        sum_qkv,
        qk_total,
        sum_out,
        sum_cq,
        sum_ckv,
        sum_cout,
        sum_up,
        sum_down,
        sum_final,
    )


def solution(mesh):
    rows, cols, heads = mesh.devices.shape
    fine = Mesh(
        mesh.devices.reshape(rows // 2, 2, cols // 2, 2, heads // 2, 2),
        ("x", "core", "chi", "clo", "zh", "zl"),
    )
    rows, cols, heads = ("x", "core"), ("chi", "clo"), ("zh", "zl")
    in_specs = (
        P(None, None, rows, cols),
        P(None, rows, cols, None),
        P(),
        P(None, rows, cols),
        P(),
        P(),
        P(),
        P(),
        P(),
        P(None, None, heads),
        P(),
        P(heads, None),
        P(None, heads),
        P(None, None, heads),
        P(heads, None),
        P(None, heads),
        P(heads, None),
        P(),
        P(None, None, rows, cols),
    )
    out_specs = (
        P(None, None, rows, cols),
        P(None, None, rows, cols),
        P(None, rows, cols, None),
        P(None, TILES),
        P(),
        P(TILES, None),
        P(),
        P(None, TILES, heads),
        P(),
        P(heads, TILES),
        P(TILES, heads),
        P(None, TILES, heads),
        P(heads, TILES),
        P(TILES, heads),
        P(heads, TILES),
        P(TILES, None),
    )
    return jax.shard_map(shards, mesh=fine, in_specs=in_specs, out_specs=out_specs, check_vma=False)
```

```python
import functools
import math

import jax
import jax.numpy as jnp
from jax import lax
from jax.experimental import pallas as pl
from jax.experimental.pallas import tpu as pltpu
from jax.sharding import Mesh, PartitionSpec as P

EPSILON = 1e-06
LOG2E = 1.4426950408889634


TILES = ("x", "core", "chi", "clo")
SHARERS = ("x", "core", "clo")
EVERYONE = ("x", "core", "chi", "clo", "zh", "zl")


def swapped(value, axis):
    return lax.ppermute(value, axis, [(i, i ^ 1) for i in range(lax.axis_size(axis))])


def from_behind(value, axis, by):
    devices = math.prod(lax.axis_size(name) for name in axis)
    pairs = [(i, i + by) for i in range(devices) if 0 <= i + by < devices]
    return lax.ppermute(value, axis, pairs)


def pick(values, index, axis):
    return lax.dynamic_index_in_dim(values, index, axis, keepdims=False)


def after(value, others):
    return lax.optimization_barrier((value, others))[0]


def sharer_slice(weight):
    sharers = math.prod(lax.axis_size(axis) for axis in SHARERS)
    depth = weight.shape[0] // sharers
    return lax.dynamic_slice_in_dim(weight, lax.axis_index(SHARERS) * depth, depth, 0)


def tile_sums(parts):
    axes = ("x", "core", "chi", "clo")
    sizes = [lax.axis_size(axis) for axis in axes]
    tiles = math.prod(sizes)
    blocks = [part.reshape(*sizes, part.shape[0] // tiles, part.shape[1]) for part in parts]

    def halved(blocks, axis, at):
        here = lax.axis_index(axis)
        sent = jnp.concatenate([pick(block, 1 - here, at) for block in blocks], -2)
        kept = jnp.concatenate([pick(block, here, at) for block in blocks], -2)
        total = kept.astype(jnp.float32) + swapped(sent, axis).astype(jnp.float32)
        return lax.reduce_precision(total, 8, 7).astype(jnp.bfloat16)

    by_core = halved(blocks, "core", 1)
    by_x = halved([by_core], "x", 0)
    by_cols = halved([by_x], "clo", 1)
    if sizes[2] == 1:
        return by_core, by_x, by_cols[0]
    return by_core, by_x, lax.psum_scatter(by_cols, "chi", scatter_dimension=0, tiled=False)


def axes_sum(values, axes):
    for axis in axes:
        values = values + swapped(values, axis)
    return values if lax.axis_size("chi") == 1 else lax.psum(values, "chi")


def from_corner(value):
    sizes = [lax.axis_size(axis) for axis in ("x", "core", "chi", "clo")]
    rows, cols = sizes[0] * sizes[1], sizes[2] * sizes[3]
    pairs = [
        ((i + 1) * cols + j + 1, i * cols + j) for i in range(rows - 1) for j in range(cols - 1)
    ]
    return lax.ppermute(value, ("x", "core", "chi", "clo"), pairs)


def partner_shard(weight, earlier):
    piece = swapped(sharer_slice(weight), "zh")
    return lax.all_gather(after(piece, earlier), SHARERS, axis=0, tiled=True)


def to_core(value):
    return swapped(value, "core")


def to_side(value):
    return swapped(value, "clo")


def to_corner(value):
    pairs = [(i, 3 - i) for i in range(4)]
    return lax.ppermute(value, ("core", "clo"), pairs)


PARTNERS = (to_core, to_side, to_corner)


def pair_sum(partial, meanwhile=()):
    mine = lax.optimization_barrier(partial.astype(jnp.bfloat16))
    other = after(swapped(mine, "zl"), meanwhile)
    return mine.astype(jnp.float32) + other.astype(jnp.float32)


def norm_rows(values):
    center = values - jnp.mean(values, -1, keepdims=True)
    spread = jnp.mean(center * center, -1, keepdims=True)
    return center * lax.rsqrt(spread + EPSILON)


def scaled_norm(values, gain):
    return norm_rows(values) * gain


def rope_tables(row_pos, col_pos, head_dim):
    quarter = head_dim // 4
    freqs = 10000.0 ** (-jnp.arange(quarter, dtype=jnp.float32) / quarter)
    row_angle = row_pos.astype(jnp.float32)[:, None] * freqs[None, :]
    col_angle = col_pos.astype(jnp.float32)[:, None] * freqs[None, :]
    cosine = jnp.concatenate(
        [jnp.cos(row_angle), jnp.cos(row_angle), jnp.cos(col_angle), jnp.cos(col_angle)], -1
    )
    sine = jnp.concatenate(
        [jnp.sin(row_angle), jnp.sin(row_angle), jnp.sin(col_angle), jnp.sin(col_angle)], -1
    )
    return (cosine, sine)


def project(left, right):
    return jnp.dot(left, right, preferred_element_type=jnp.float32)


def outer_sum(left, right):
    return jnp.einsum("rd,re->de", left, right, preferred_element_type=jnp.float32)


def back_dot(grads, weight):
    return jnp.einsum("re,de->rd", grads, weight, preferred_element_type=jnp.float32)


def float_dot(left, right, parts=2):
    total = jnp.zeros((left.shape[0], right.shape[1]), jnp.float32)
    for _ in range(parts):
        part = left.astype(jnp.bfloat16)
        total += jnp.dot(part, right, preferred_element_type=jnp.float32)
        left = left - part.astype(jnp.float32)
    return total


def dot_rows(left, right):
    return lax.dot_general(left, right, (((1,), (1,)), ((), ())), preferred_element_type=jnp.float32)


def dot_cols(left, right):
    return lax.dot_general(left, right, (((0,), (0,)), ((), ())), preferred_element_type=jnp.float32)


def head_hat(values, same, head_dim):
    center = values - float_dot(values, same, 3) * (1.0 / head_dim)
    spread = float_dot(center * center, same) * (1.0 / head_dim)
    scale = lax.rsqrt(spread + EPSILON)
    return center * scale, scale


def head_hat_back(hat, scale, grads, same, head_dim):
    mean = float_dot(grads, same) * (1.0 / head_dim)
    along = float_dot(grads * hat, same) * (1.0 / head_dim)
    return scale * (grads - mean - hat * along)


def accumulate(ref, value):
    @pl.when(pl.program_id(0) == 0)
    def _():
        ref[...] = jnp.zeros_like(ref)

    ref[...] += value


def turn_kernel(head_dim, proj, cosine, sine, gains, same, turn, queries, near):
    for part in range(2):
        hat, _ = head_hat(proj[part], same[...], head_dim)
        scaled = hat * gains[part : part + 1]
        turned = scaled * cosine[...] + float_dot(scaled, turn[...]) * sine[...]
        if part == 0:
            queries[0] = turned.astype(queries.dtype)
        else:
            near[0, 0] = turned.astype(near.dtype)
    near[1, 0] = proj[2].astype(near.dtype)


def turn_back_kernel(
    head_dim, proj, grad_q, own, one, two, three, cosine, sine, gains, same, back, grads, gain_sums
):
    sums = []
    for part in range(2):
        if part == 0:
            grad = grad_q[0]
        else:
            grad = own[0, 0] + one[0, 0].astype(jnp.float32)
            grad = grad + two[0, 0].astype(jnp.float32) + three[0, 0].astype(jnp.float32)
        hat, scale = head_hat(proj[part], same[...], head_dim)
        grad = grad * cosine[...] + float_dot(grad * sine[...], back[...])
        sums.append(jnp.sum(grad * hat, 0, keepdims=True))
        grad = head_hat_back(hat, scale, grad * gains[part : part + 1], same[...], head_dim)
        grads[part] = grad.astype(grads.dtype)
    grad = own[1, 0] + one[1, 0].astype(jnp.float32)
    grad = grad + two[1, 0].astype(jnp.float32) + three[1, 0].astype(jnp.float32)
    grads[2] = grad.astype(grads.dtype)
    accumulate(gain_sums, jnp.concatenate(sums + [jnp.zeros((6, sums[0].shape[1]), jnp.float32)], 0))


def attend_kernel(heads, scaling, queries, near_a, near_b, near_c, near_d, masks, mixture, totals):
    nears = (near_a, near_b, near_c, near_d)
    lane = lax.broadcasted_iota(jnp.int32, totals.shape[1:], 1)
    mixed = jnp.zeros(mixture.shape[1:], jnp.float32)
    logs = jnp.zeros(totals.shape[1:], jnp.float32)
    for head in range(heads):
        mask = masks[head : head + 1]
        query = queries[0] * mask
        scores = [dot_rows(query, near[0, 0]) for near in nears]
        highest = functools.reduce(jnp.maximum, [jnp.max(s, -1, keepdims=True) for s in scores])
        expo = [jnp.exp2(s * (scaling * LOG2E) - highest * (scaling * LOG2E)) for s in scores]
        total = functools.reduce(jnp.add, [jnp.sum(e, -1, keepdims=True) for e in expo])
        inverse = 1.0 / total
        parts = [
            jnp.dot(e.astype(jnp.bfloat16), near[1, 0] * mask, preferred_element_type=jnp.float32)
            for e, near in zip(expo, nears)
        ]
        mixed += functools.reduce(jnp.add, parts) * inverse
        logs = jnp.where(lane == head, highest * scaling + jnp.log(total), logs)
    mixture[0] = mixed.astype(mixture.dtype)
    totals[0] = logs


def attend_back_kernel(
    heads,
    scaling,
    queries,
    near_a,
    near_b,
    near_c,
    near_d,
    masks,
    totals,
    grad_mix,
    grad_q,
    grad_a,
    grad_b,
    grad_c,
    grad_d,
    sums,
):
    nears = (near_a, near_b, near_c, near_d)
    lane = lax.broadcasted_iota(jnp.int32, totals.shape[1:], 1)
    grad_query = jnp.zeros(grad_q.shape[1:], jnp.float32)
    for head in range(heads):
        mask = masks[head : head + 1]
        query = queries[0] * mask
        grad_out = grad_mix[0] * mask
        log_total = jnp.sum(jnp.where(lane == head, totals[0], 0.0), -1, keepdims=True)
        log_total = log_total * LOG2E
        scores = [dot_rows(query, near[0, 0]) * (scaling * LOG2E) for near in nears]
        weights = [jnp.exp2(score - log_total) for score in scores]
        grad_w = [dot_rows(grad_out, near[1, 0]) for near in nears]
        inner = functools.reduce(
            jnp.add, [jnp.sum(w * g, -1, keepdims=True) for w, g in zip(weights, grad_w)]
        )
        for at, near in enumerate(nears):
            grad_scores = (weights[at] * (grad_w[at] - inner)).astype(jnp.bfloat16)
            grad_query += jnp.dot(grad_scores, near[0, 0] * mask, preferred_element_type=jnp.float32)
            grad_key = dot_cols(grad_scores, query)
            grad_value = dot_cols(weights[at].astype(jnp.bfloat16), grad_out)
            if head == 0:
                sums[at, 0] = grad_key
                sums[at, 1] = grad_value
            else:
                sums[at, 0] += grad_key
                sums[at, 1] += grad_value
    grad_q[0] = grad_query * scaling
    for at, out in enumerate((grad_a, grad_b, grad_c, grad_d)):
        out[0, 0] = (sums[at, 0] * scaling).astype(out.dtype)
        out[1, 0] = sums[at, 1].astype(out.dtype)


def text_kernel(head_dim, text, gains, same, keys_values):
    for group in range(2):
        hat, _ = head_hat(text[group, 0, 0], same[...], head_dim)
        keys_values[group, 0, 0] = (hat * gains[1:2]).astype(keys_values.dtype)
        keys_values[group, 1, 0] = text[group, 1, 0].astype(keys_values.dtype)


def text_back_kernel(head_dim, text, grads, gains, same, grad_text, gain_sums):
    width = grad_text.shape[4]
    gain_k = jnp.zeros((1, width), jnp.float32)
    for group in range(2):
        hat, scale = head_hat(text[group, 0, 0], same[...], head_dim)
        grad = grads[group, 0, 0]
        gain_k += jnp.sum(grad * hat, 0, keepdims=True)
        grad = head_hat_back(hat, scale, grad * gains[1:2], same[...], head_dim)
        grad_text[group, 0, 0] = grad.astype(grad_text.dtype)
        grad_text[group, 1, 0] = grads[group, 1, 0].astype(grad_text.dtype)
    accumulate(gain_sums, jnp.concatenate([gain_k, jnp.zeros((7, width), jnp.float32)], 0))


def cross_kernel(heads, head_dim, scaling, pre, text, present, gains, same, masks, mixture, totals):
    lane = lax.broadcasted_iota(jnp.int32, totals.shape[2:], 1)
    allowed = present[0] > 0
    for group in range(2):
        hat, _ = head_hat(pre[group, 0], same[...], head_dim)
        queries = (hat * gains[0:1]).astype(jnp.bfloat16)
        keys, values = text[group, 0, 0], text[group, 1, 0]
        mixed = jnp.zeros(mixture.shape[2:], jnp.float32)
        logs = jnp.zeros(totals.shape[2:], jnp.float32)
        for head in range(heads):
            mask = masks[head : head + 1]
            scores = jnp.where(allowed, dot_rows(queries * mask, keys) * scaling, -1e30)
            highest = jnp.max(scores, -1, keepdims=True)
            expo = jnp.exp(scores - highest)
            total = jnp.sum(expo, -1, keepdims=True)
            weights = (expo * (1.0 / total)).astype(jnp.bfloat16)
            mixed += jnp.dot(weights, values * mask, preferred_element_type=jnp.float32)
            logs = jnp.where(lane == head, highest + jnp.log(total), logs)
        mixture[group, 0] = mixed.astype(mixture.dtype)
        totals[group, 0] = logs


def cross_back_kernel(
    heads,
    head_dim,
    scaling,
    pre,
    text,
    present,
    gains,
    same,
    masks,
    totals,
    grad_mix,
    grad_pre,
    grad_text,
    gain_sums,
):
    lane = lax.broadcasted_iota(jnp.int32, totals.shape[2:], 1)
    allowed = present[0] > 0
    width = grad_pre.shape[3]
    gain_q = jnp.zeros((1, width), jnp.float32)
    for group in range(2):
        q_hat, q_scale = head_hat(pre[group, 0], same[...], head_dim)
        queries = (q_hat * gains[0:1]).astype(jnp.bfloat16)
        keys, values = text[group, 0, 0], text[group, 1, 0]
        grad_q = jnp.zeros(grad_pre.shape[2:], jnp.float32)
        for head in range(heads):
            mask = masks[head : head + 1]
            query = queries * mask
            grad_out = grad_mix[group, 0] * mask
            log_total = jnp.sum(jnp.where(lane == head, totals[group, 0], 0.0), -1, keepdims=True)
            scores = jnp.where(allowed, dot_rows(query, keys) * scaling, -1e30)
            weights = jnp.exp(scores - log_total)
            grad_w = dot_rows(grad_out, values)
            inner = jnp.sum(weights * grad_w, -1, keepdims=True)
            grad_scores = (weights * (grad_w - inner)).astype(jnp.bfloat16)
            grad_q += jnp.dot(grad_scores, keys * mask, preferred_element_type=jnp.float32)
            grad_k = dot_cols(grad_scores, query) * scaling
            grad_v = dot_cols(weights.astype(jnp.bfloat16), grad_out)
            if head == 0:
                grad_text[group, 0, 0] = grad_k
                grad_text[group, 1, 0] = grad_v
            else:
                grad_text[group, 0, 0] += grad_k
                grad_text[group, 1, 0] += grad_v
        grad_q = grad_q * scaling
        gain_q += jnp.sum(grad_q * q_hat, 0, keepdims=True)
        grad_q = head_hat_back(q_hat, q_scale, grad_q * gains[0:1], same[...], head_dim)
        grad_pre[group, 0] = grad_q.astype(grad_pre.dtype)
    accumulate(gain_sums, jnp.concatenate([gain_q, jnp.zeros((7, width), jnp.float32)], 0))


def whole(array):
    rank = len(array.shape)
    return pl.BlockSpec(array.shape, lambda pack: (0,) * rank)


def by_pack(array, axis, depth=1):
    shape = array.shape[:axis] + (depth,) + array.shape[axis + 1 :]
    rank = len(shape)
    return pl.BlockSpec(shape, lambda pack: tuple(pack if at == axis else 0 for at in range(rank)))


def per_pack(body, packs, inputs, outputs, flops, scratch=()):
    ins, in_specs, out_specs, shapes = [], [], [], []
    for array, axis, depth in inputs:
        ins.append(array)
        in_specs.append(whole(array) if axis is None else by_pack(array, axis, depth))
    for shape, dtype, axis, depth in outputs:
        spec = jax.ShapeDtypeStruct(shape, dtype)
        shapes.append(spec)
        out_specs.append(whole(spec) if axis is None else by_pack(spec, axis, depth))
    moved = sum(math.prod(a.shape) * a.dtype.itemsize for a in ins + shapes)
    return pl.pallas_call(
        body,
        grid=(packs,),
        in_specs=in_specs,
        out_specs=out_specs,
        out_shape=shapes,
        scratch_shapes=scratch,
        cost_estimate=pl.CostEstimate(flops=flops, bytes_accessed=moved, transcendentals=0),
        compiler_params=pltpu.CompilerParams(
            dimension_semantics=("arbitrary",), vmem_limit_bytes=48 * 1024 * 1024
        ),
    )(*ins)


def shards(
    latent,
    skip_in,
    context,
    image_ids,
    text_mask,
    patch_weight,
    skip_gain,
    skip_weight,
    norm_gains,
    qkv_weight,
    qk_gains,
    out_weight,
    cq_weight,
    ckv_weight,
    cout_weight,
    up_weight,
    down_weight,
    final_weight,
    cotangent,
):
    pack_count = latent.shape[0]
    in_channels = latent.shape[1]
    out_channels = cotangent.shape[1]
    tile_side = image_ids.shape[1]
    cells = tile_side * tile_side
    row_total = pack_count * cells
    model_width = skip_weight.shape[1]
    head_dim = qk_gains.shape[1]
    true_width = qkv_weight.shape[2]
    local_heads = true_width // head_dim
    head_width = -(-true_width // 128) * 128
    spare = head_width - true_width
    both_channels = in_channels + out_channels
    half_cells = cells // 2
    quarter_cells = cells // 4
    half_total = row_total // 2
    quarter_total = row_total // 4
    text_width = context.shape[2]
    tiles = math.prod(lax.axis_size(axis) for axis in TILES)
    upper, lower = lax.axis_index("zh"), lax.axis_index("zl")
    scaling = 1.0 / math.sqrt(head_dim)
    bf16 = jnp.bfloat16

    def my_half(values):
        shape = values.shape[1:]
        cut = pick(values.reshape(pack_count, 2, half_cells, *shape), upper, 1)
        return cut.reshape(half_total, *shape)

    def other_half(values):
        shape = values.shape[1:]
        cut = pick(values.reshape(pack_count, 2, half_cells, *shape), 1 - upper, 1)
        return cut.reshape(half_total, *shape)

    def both_halves(mine, other):
        shape = mine.shape[1:]
        mine = mine.reshape(pack_count, half_cells, *shape)
        other = other.reshape(pack_count, half_cells, *shape)
        first = jnp.where(upper == 0, mine, other)
        second = jnp.where(upper == 0, other, mine)
        return jnp.stack([first, second], 1).reshape(row_total, *shape)

    stacked = jnp.concatenate([latent, cotangent], 1)
    rows_axes, cols_axes = ("x", "core"), ("chi", "clo")
    lower_rim = from_behind(stacked[:, :, :1, :], rows_axes, -1)
    right_rim = from_behind(stacked[:, :, :, :1], cols_axes, -1)
    corner = from_corner(stacked[:, :, :1, :1])
    lower_rim = jnp.concatenate([lower_rim, corner], 3)[:, :, :, 1:]
    stacked = jnp.concatenate([stacked, right_rim], 3)[:, :, 1:, 1:]
    stacked = jnp.concatenate([stacked, lower_rim], 2)
    pieces = stacked.reshape(pack_count, both_channels, tile_side, 2, tile_side, 2)
    pieces = pieces.transpose(0, 2, 4, 1, 3, 5).reshape(row_total, both_channels * 4)
    patches = pieces[:, : in_channels * 4]
    grad_result = my_half(pieces[:, in_channels * 4 :])

    def spread_heads(values):
        return jnp.pad(jnp.tile(values, (1, local_heads)), ((0, 0), (0, spare)))

    qkv_wide = jnp.pad(qkv_weight, ((0, 0), (0, 0), (0, spare)))
    ckv_wide = jnp.pad(ckv_weight, ((0, 0), (0, 0), (0, spare)))
    out_tall, cout_tall, cq_tall = [
        jnp.pad(weight, ((0, spare), (0, 0))) for weight in (out_weight, cout_weight, cq_weight.T)
    ]
    token_index = jnp.arange(cells, dtype=jnp.int32)
    row_pos = lax.axis_index("core") * tile_side + token_index // tile_side
    col_pos = lax.axis_index("clo") * tile_side + token_index % tile_side
    cosine, sine = rope_tables(row_pos, col_pos, head_dim)
    cosine, sine = spread_heads(cosine), spread_heads(sine)
    lanes = jnp.arange(head_width, dtype=jnp.int32)
    head_of, place = lanes // head_dim, lanes % head_dim
    same = (head_of[:, None] == head_of[None, :]).astype(bf16)
    quarter = head_dim // 4
    ahead = (place // quarter % 2 == 0)[None, :]
    turn = jnp.where(
        ahead,
        -(lanes[:, None] == lanes[None, :] + quarter).astype(bf16),
        (lanes[:, None] == lanes[None, :] - quarter).astype(bf16),
    )
    masks = (jnp.arange(8, dtype=jnp.int32)[:, None] == head_of[None, :]).astype(bf16)
    flat_gains = spread_heads(jnp.pad(qk_gains, ((0, 4), (0, 0))))
    self_gains, cross_gains = flat_gains, jnp.roll(flat_gains, -2, 0)

    embed = project(patches, patch_weight)
    joined = jnp.concatenate(
        [embed, skip_in.reshape(row_total, model_width).astype(jnp.float32)], 1
    )
    normed = scaled_norm(joined, skip_gain).astype(bf16)
    slices = [sharer_slice(weight) for weight in (out_tall, cout_tall, cq_tall)]
    moved = swapped(jnp.stack(slices), "zh")
    gathered = lax.all_gather(after(moved, normed), SHARERS, axis=0, tiled=False)
    out_other, cout_other, cq_other = [
        gathered[:, at].reshape(head_width, model_width) for at in range(3)
    ]
    hidden = project(normed, skip_weight)
    ckv_other = partner_shard(ckv_wide.reshape(2 * text_width, head_width), hidden)
    out_pair = (out_tall, out_other)
    cq_pair = (cq_tall, cq_other)
    ckv_pair = (ckv_wide, ckv_other.reshape(ckv_wide.shape))
    cout_pair = (cout_tall, cout_other)
    n_one = scaled_norm(hidden, norm_gains[0]).astype(bf16)
    projected = jnp.einsum("rd,sde->sre", n_one, qkv_wide, preferred_element_type=jnp.float32)
    tile_flat = (pack_count, cells, head_width)
    near_flat = (2, pack_count, cells, head_width)
    queries, near_own = per_pack(
        functools.partial(turn_kernel, head_dim),
        pack_count,
        [
            (projected, 1, cells),
            (cosine, None, 1),
            (sine, None, 1),
            (self_gains, None, 1),
            (same, None, 1),
            (turn, None, 1),
        ],
        [(tile_flat, bf16, 0, 1), (near_flat, bf16, 1, 1)],
        row_total * head_width * head_width * 36,
    )
    nears = (near_own,) + tuple(to_partners(near_own) for to_partners in PARTNERS)
    up_both = jnp.concatenate([after(up_weight, nears[1]), partner_shard(up_weight, near_own)], 1)
    down_both = jnp.concatenate([after(down_weight, nears[1]), partner_shard(down_weight, near_own)], 0)
    near_args = [(near, 1, 1) for near in nears]
    self_flops = row_total * 4 * cells * head_width * local_heads * 4
    mixture, self_totals = per_pack(
        functools.partial(attend_kernel, local_heads, scaling),
        pack_count,
        [(queries, 0, 1), *near_args, (masks, None, 1)],
        [(tile_flat, bf16, 0, 1), ((pack_count, cells, 128), jnp.float32, 0, 1)],
        self_flops,
    )
    mixture = mixture.reshape(row_total, head_width)
    mix_pair = (my_half(mixture), swapped(other_half(mixture), "zh"))

    def joint(lefts, rights):
        return project(lefts[0], rights[0]) + project(lefts[1], rights[1])

    def joint_back(grads, weights):
        return back_dot(grads[0], weights[0]) + back_dot(grads[1], weights[1])

    x_one = my_half(hidden) + pair_sum(joint(mix_pair, out_pair))
    n_two = scaled_norm(x_one, norm_gains[1]).astype(bf16)
    caption = after(image_ids[:, 0, 0], near_own)
    text_len = context.shape[1]
    padding = -text_len % 128
    padded_len = text_len + padding
    chosen = jnp.pad(context[caption], ((0, 0), (0, padding), (0, 0)))
    present = jnp.pad((text_mask[caption] > 0).astype(jnp.float32), ((0, 0), (0, padding)))
    present = present[:, None, :]
    text_pre = jnp.stack(
        [
            jnp.einsum("ptc,sce->spte", chosen, weight, preferred_element_type=jnp.float32)
            for weight in ckv_pair
        ]
    )
    cross_pre = jnp.stack([back_dot(n_two, weight) for weight in cq_pair])
    cross_pre = cross_pre.reshape(2, pack_count, half_cells, head_width)
    (text_near,) = per_pack(
        functools.partial(text_kernel, head_dim),
        pack_count,
        [(text_pre, 2, 1), (cross_gains, None, 1), (same, None, 1)],
        [(text_pre.shape, bf16, 2, 1)],
        text_pre.size * head_width * 4,
    )
    cross_args = [
        (cross_pre, 1, 1),
        (text_near, 2, 1),
        (present, 0, 1),
        (cross_gains, None, 1),
        (same, None, 1),
        (masks, None, 1),
    ]
    cross_flat = (2, pack_count, half_cells, head_width)
    cross_flops = half_total * padded_len * head_width * local_heads * 8
    cross_mix, cross_totals = per_pack(
        functools.partial(cross_kernel, local_heads, head_dim, scaling),
        pack_count,
        cross_args,
        [(cross_flat, bf16, 1, 1), ((2, pack_count, half_cells, 128), jnp.float32, 1, 1)],
        cross_flops,
    )
    cross_mixes = [cross_mix[group].reshape(half_total, head_width) for group in range(2)]
    x_two = x_one + pair_sum(joint(cross_mixes, cout_pair))
    n_three = scaled_norm(x_two, norm_gains[2]).astype(bf16)
    up_pre = project(n_three, up_both)
    act = jax.nn.gelu(up_pre, approximate=True).astype(bf16)
    x_three = x_two + pair_sum(project(act, down_both))
    n_four = norm_rows(x_three).astype(bf16)
    result = project(n_four, final_weight).astype(bf16)
    result = both_halves(result, swapped(result, "zh"))
    grad_final = outer_sum(n_four, grad_result)
    unused, pull = jax.vjp(norm_rows, x_three)
    grad_stream = pull(back_dot(grad_result, final_weight))[0]
    branch = grad_stream.astype(bf16)
    unused, pull = jax.vjp(functools.partial(jax.nn.gelu, approximate=True), up_pre)
    grad_up_pre = pull(back_dot(branch, down_both))[0].astype(bf16)
    grad_down = outer_sum(branch, act).astype(bf16)
    grad_up = outer_sum(n_three, grad_up_pre).astype(bf16)
    grad_n_three = pair_sum(back_dot(grad_up_pre, up_both), (grad_down, grad_up))

    def scattered(grads):
        return lax.psum_scatter(grads, TILES, scatter_dimension=0, tiled=True)

    mlp_shares = (scattered(grad_down), scattered(grad_up))
    unused, pull = jax.vjp(scaled_norm, x_two, norm_gains[2])
    grad_input, gain_three = pull(grad_n_three)
    grad_stream = grad_stream + grad_input
    branch = grad_stream.astype(bf16)
    grad_cmix = jnp.stack([back_dot(branch, weight).astype(bf16) for weight in cout_pair])
    grad_cq, grad_text, cross_sums = per_pack(
        functools.partial(cross_back_kernel, local_heads, head_dim, scaling),
        pack_count,
        [*cross_args, (cross_totals, 1, 1), (grad_cmix.reshape(cross_flat), 1, 1)],
        [
            (cross_flat, bf16, 1, 1),
            (text_pre.shape, jnp.float32, 2, 1),
            ((8, head_width), jnp.float32, None, 1),
        ],
        3 * cross_flops,
    )
    grad_cqs = [grad_cq[group].reshape(half_total, head_width) for group in range(2)]
    grad_couts = [outer_sum(branch, mix).astype(bf16) for mix in cross_mixes]
    grad_cq_ws = [outer_sum(n_two, grad).astype(bf16) for grad in grad_cqs]
    grad_n_two = pair_sum(
        project(grad_cqs[0], cq_pair[0]) + project(grad_cqs[1], cq_pair[1]),
        (grad_couts, grad_cq_ws),
    )
    grad_text, text_sums = per_pack(
        functools.partial(text_back_kernel, head_dim),
        pack_count,
        [(text_pre, 2, 1), (grad_text, 2, 1), (cross_gains, None, 1), (same, None, 1)],
        [(text_pre.shape, bf16, 2, 1), ((8, head_width), jnp.float32, None, 1)],
        text_pre.size * head_width * 8,
    )
    grad_ckvs = [
        jnp.einsum(
            "ptc,pte->ce", chosen, grad_text[group, side], preferred_element_type=jnp.float32
        ).astype(bf16)
        for group in range(2)
        for side in range(2)
    ]
    narrow = grad_final.astype(bf16).reshape(tiles, -1, 4 * out_channels).transpose(0, 2, 1)
    narrow = jnp.pad(narrow, ((0, 0), (0, 0), (0, head_width - narrow.shape[2])))
    narrow = narrow.reshape(-1, head_width)
    mine = [grad_couts[0], grad_cq_ws[0], grad_ckvs[0], grad_ckvs[1]]
    other = [grad_couts[1], grad_cq_ws[1], grad_ckvs[2], grad_ckvs[3]]
    cross_steps = tile_sums(mine + [narrow] + other)
    cross_shares = cross_steps[2]
    unused, pull = jax.vjp(scaled_norm, x_one, norm_gains[1])
    grad_input, gain_two = pull(grad_n_two)
    grad_stream = grad_stream + grad_input
    branch = grad_stream.astype(bf16)
    grad_amixes = [back_dot(branch, weight).astype(bf16) for weight in out_pair]
    grad_amix = both_halves(grad_amixes[0], swapped(grad_amixes[1], "zh"))
    grad_outs = [outer_sum(branch, mix).astype(bf16) for mix in mix_pair]
    down_mine, down_other = jnp.split(mlp_shares[0], 2, 1)
    up_mine, up_other = jnp.split(mlp_shares[1], 2, 1)
    down_other, up_other = [swapped(after(x, grad_amix), "zh") for x in (down_other, up_other)]
    grad_q, *grad_nears = per_pack(
        functools.partial(attend_back_kernel, local_heads, scaling),
        pack_count,
        [
            (queries, 0, 1),
            *near_args,
            (masks, None, 1),
            (self_totals, 0, 1),
            (after(grad_amix.reshape(tile_flat), cross_steps[0]), 0, 1),
        ],
        [(tile_flat, jnp.float32, 0, 1), (near_flat, jnp.float32, 1, 1)]
        + [(near_flat, bf16, 1, 1)] * 3,
        self_flops * 5 // 2,
        [pltpu.VMEM((4, 2, cells, head_width), jnp.float32)],
    )
    arrived = [to_partners(grad) for to_partners, grad in zip(PARTNERS, grad_nears[1:])]
    arrived = after(arrived, (down_other, up_other, grad_outs, cross_steps[1]))
    grad_proj, self_sums = per_pack(
        functools.partial(turn_back_kernel, head_dim),
        pack_count,
        [
            (projected, 1, cells),
            (grad_q, 0, 1),
            (grad_nears[0], 1, 1),
            *[(grad, 1, 1) for grad in arrived],
            (cosine, None, 1),
            (sine, None, 1),
            (self_gains, None, 1),
            (same, None, 1),
            (turn.T, None, 1),
        ],
        [(projected.shape, bf16, 1, cells), ((8, head_width), jnp.float32, None, 1)],
        row_total * head_width * head_width * 60,
    )
    grad_n_one = jnp.einsum("sre,sde->rd", grad_proj, qkv_wide, preferred_element_type=jnp.float32)
    grad_qkvs = [outer_sum(n_one, grad_proj[part]).astype(bf16) for part in range(3)]
    self_steps = tile_sums(grad_outs + grad_qkvs)
    self_shares = self_steps[2]
    fine = grad_n_one.astype(bf16).reshape(pack_count, 2, 2, quarter_cells, model_width)
    kept = pick(fine, lower, 2).astype(jnp.float32)
    facing = after(swapped(pick(fine, 1 - lower, 2), "zl"), (grad_qkvs, cross_shares))
    kept = kept + facing.astype(jnp.float32)
    sent = swapped(pick(kept, 1 - upper, 1).astype(bf16), "zh")
    sent = after(sent, self_steps[0]).astype(jnp.float32)
    grad_n_one = (pick(kept, upper, 1) + sent).reshape(quarter_total, model_width)

    def my_quarter(half_rows):
        cut = pick(half_rows.reshape(pack_count, 2, quarter_cells, model_width), lower, 1)
        return cut.reshape(quarter_total, model_width)

    unused, pull = jax.vjp(scaled_norm, my_quarter(my_half(hidden)), norm_gains[0])
    grad_input, gain_one = pull(grad_n_one)
    branch = (my_quarter(grad_stream) + grad_input).astype(bf16)
    quarter = branch.reshape(pack_count, quarter_cells, model_width)

    def in_order(mine, other, index, axis):
        first = jnp.where(index == 0, mine, other)
        second = jnp.where(index == 0, other, mine)
        return jnp.stack([first, second], axis)

    branch = in_order(quarter, swapped(quarter, "zh"), upper, 1)
    facing = after(swapped(branch, "zl"), self_steps[1])
    branch = in_order(branch, facing, lower, 2).reshape(row_total, model_width)

    share_at = (2 * upper + lower) * true_width
    my_share = lax.dynamic_slice_in_dim(branch, share_at, true_width, 1)
    my_share = jnp.pad(my_share, ((0, 0), (0, spare)))
    grad_skip_w = outer_sum(normed, my_share).astype(bf16)
    skip_steps = tile_sums([grad_skip_w])
    skip_shares = skip_steps[2]
    branch = after(branch, grad_skip_w)
    unused, pull = jax.vjp(scaled_norm, joined, skip_gain)
    grad_joined, gain_skip = pull(after(back_dot(branch, skip_weight), skip_steps[0]))
    grad_skip = grad_joined[:, model_width:].astype(bf16).reshape(skip_in.shape)
    grad_embed = grad_joined[:, :model_width].astype(bf16)
    grad_patch_w = outer_sum(grad_embed, patches)
    grad_patches = back_dot(grad_embed, patch_weight).astype(bf16)
    def with_partner(mine, other):
        other = after(swapped(after(other, branch), "zh"), gain_skip)
        return mine.astype(jnp.float32) + other.astype(jnp.float32)

    tile_rows = model_width // tiles
    sum_down = (down_mine.astype(jnp.float32) + down_other.astype(jnp.float32)).T
    sum_up = up_mine.astype(jnp.float32) + up_other.astype(jnp.float32)
    narrow_rows = 4 * out_channels
    near_rows = (cross_shares.shape[0] - narrow_rows) // 2
    far = [cross_shares[near_rows + narrow_rows :], cross_shares[near_rows:-near_rows]]
    cross_total = with_partner(cross_shares[:-near_rows], jnp.concatenate(far, 0))
    sum_cout = cross_total[:tile_rows, :true_width].T
    sum_cq = cross_total[tile_rows : 2 * tile_rows, :true_width]
    sum_final = cross_total[-4 * out_channels :, :tile_rows].T
    sum_ckv = cross_total[2 * tile_rows : -4 * out_channels, :true_width].reshape(
        2, -1, true_width
    )
    sum_out = with_partner(self_shares[:tile_rows], self_shares[tile_rows : 2 * tile_rows])
    sum_out = sum_out[:, :true_width].T
    sum_qkv = self_shares[2 * tile_rows :, :true_width].astype(jnp.float32)
    sum_qkv = sum_qkv.reshape(3, tile_rows, true_width)
    placed = jnp.concatenate([result, grad_patches], 1)
    placed = placed.reshape(pack_count, tile_side, tile_side, both_channels, 2, 2).transpose(
        0, 3, 1, 4, 2, 5
    )
    placed = placed.reshape(pack_count, both_channels, 2 * tile_side, 2 * tile_side)
    placed = jnp.pad(placed, ((0, 0), (0, 0), (1, 0), (1, 0)))
    moved_cols = from_behind(placed[:, :, :, -1:], ("chi", "clo"), 1)
    placed = jnp.concatenate([moved_cols, placed[:, :, :, 1:-1]], 3)
    moved_rows = from_behind(placed[:, :, -1:, :], ("x", "core"), 1)
    placed = jnp.concatenate([moved_rows, placed[:, :, 1:-1, :]], 2)
    out_latent = placed[:, :out_channels]
    grad_latent = placed[:, out_channels:]
    qk_parts = jnp.concatenate([self_sums[:2], cross_sums[:1], text_sums[:1]], 0)
    qk_parts = jnp.sum(qk_parts[:, :true_width].reshape(4, local_heads, head_dim), 1).reshape(-1)
    gains = [gain_one, 0.5 * gain_two, 0.5 * gain_three]
    gains = gains + [jnp.pad(qk_parts, (0, model_width - qk_parts.shape[0]))]
    gains = axes_sum(jnp.stack(gains), ("zl", "zh", "core", "x", "clo"))
    gains_total = gains[:3]
    qk_total = gains[3, : 4 * head_dim].reshape(4, head_dim)
    skip_gain_total = axes_sum(after(gain_skip.reshape(2, -1), skip_steps[1]), ("core", "x", "clo"))
    skip_gain_total = skip_gain_total.reshape(-1)
    sum_skip = lax.all_gather(skip_shares, ("zh", "zl"), axis=0, tiled=False)
    sum_skip = sum_skip[:, :, :true_width].transpose(1, 0, 2).reshape(-1, model_width)
    sum_patch = tile_sums([grad_patch_w.astype(bf16)])[2].astype(jnp.float32).T
    return (
        out_latent,
        grad_latent,
        grad_skip,
        sum_patch,
        skip_gain_total,
        sum_skip.astype(jnp.float32),
        gains_total,
        sum_qkv,
        qk_total,
        sum_out,
        sum_cq,
        sum_ckv,
        sum_cout,
        sum_up,
        sum_down,
        sum_final,
    )


def solution(mesh):
    rows, cols, heads = mesh.devices.shape
    fine = Mesh(
        mesh.devices.reshape(rows // 2, 2, cols // 2, 2, heads // 2, 2),
        ("x", "core", "chi", "clo", "zh", "zl"),
    )
    rows, cols, heads = ("x", "core"), ("chi", "clo"), ("zh", "zl")
    in_specs = (
        P(None, None, rows, cols),
        P(None, rows, cols, None),
        P(),
        P(None, rows, cols),
        P(),
        P(),
        P(),
        P(),
        P(),
        P(None, None, heads),
        P(),
        P(heads, None),
        P(None, heads),
        P(None, None, heads),
        P(heads, None),
        P(None, heads),
        P(heads, None),
        P(),
        P(None, None, rows, cols),
    )
    out_specs = (
        P(None, None, rows, cols),
        P(None, None, rows, cols),
        P(None, rows, cols, None),
        P(None, TILES),
        P(),
        P(TILES, None),
        P(),
        P(None, TILES, heads),
        P(),
        P(heads, TILES),
        P(TILES, heads),
        P(None, TILES, heads),
        P(heads, TILES),
        P(TILES, heads),
        P(heads, TILES),
        P(TILES, None),
    )
    return jax.shard_map(shards, mesh=fine, in_specs=in_specs, out_specs=out_specs, check_vma=False)
```
